256 devices in a mesh: row: 32 (over x, y, z_hi), col: 8 (over z_lo, core).
Axes of the slice: x: 4, y: 4, z: 8 (z_hi: 2, z_lo: 4; z = z_hi * 4 + z_lo), core: 2. Of those that a mesh axis runs over, the one named last changes fastest.
Arguments:
- preacts: bfloat16 [1024, 65536], P('col', 'row'), may hold values from -6 to 6
- resident: bfloat16 [65536, 1024], P('row', 'col'), may hold values from 0 to 0.0101
- ridge: float32 [1], replicated, may hold values from 0.5 to 2
Outputs:
- panel_factor: float32 [2, 256, 65536], P(None, 'col', 'row')
The draws below stay inside these ranges and needn't reach their ends.
All inputs are finite; a program needn't handle non-finite values.
Results may differ from the reference program's by a relative error of at most 0.0003.
Values may be sent and summed in bfloat16 or wider, within the bound.
A program may use at most 64 MiB of HBM per device.

```python
import math
import jax
import jax.numpy as jnp
from jax import lax

P_SIZE = 256
FEAT = 65536
SAMPLES = 1024
RESID = 1024


def draw_resident(key, part):
    values = jax.random.uniform(jax.random.fold_in(key, 11), (FEAT, RESID), jnp.float32) * 0.01
    return values.astype(jnp.bfloat16)


def level_of(rng, extent, shards, smallest, top_value):
    factor_of = 1.0
    for axis_at, parts in shards:
        draws = jax.random.uniform(jax.random.fold_in(jax.random.fold_in(rng, 6), axis_at), (parts,), jnp.float32, smallest / len(shards), top_value / len(shards))
        factor_of = factor_of * jnp.repeat(jnp.exp(draws), extent[axis_at] // parts).reshape((-1,) + (1,) * (len(extent) - 1 - axis_at))
    return factor_of


def centred(key, extent, width, most, cuts=(), held_as=jnp.bfloat16):
    level = level_of(key, extent, cuts, -0.22, 0.18) if cuts else 1.0
    drawn = jax.random.normal(key, extent, jnp.float32) * width * level
    return jnp.minimum(jnp.maximum(drawn, -most), most).astype(held_as)


def setup_inputs(seed: int = 0) -> dict:
    key_of = jax.random.split(jax.random.key(seed), 4)
    preacts = centred(key_of[0], (SAMPLES, FEAT), 1.0, 6.0, ((0, 8), (1, 32)))
    resident = draw_resident(jax.random.fold_in(key_of[3], 71), 0)
    ridge = jnp.clip(jnp.exp(jax.random.uniform(key_of[2], (1,), jnp.float32, math.log(0.5), math.log(2.0))), 0.5, 2.0)
    return dict(preacts=preacts, resident=resident, ridge=ridge)


def reference(preacts, resident, ridge):
    hi = lax.Precision.HIGHEST
    feats = jnp.maximum(preacts, 0).astype(jnp.float32)
    count = feats.shape[0]
    total = feats.shape[1]
    factor = resident.astype(jnp.float32)
    ids = jnp.arange(total)
    local = jnp.arange(P_SIZE)
    results = []
    previous = None
    for p in range(2):
        low = p * P_SIZE
        cols = feats[:, low:low + P_SIZE]
        strip = jnp.dot(feats.T, cols, precision=hi) / count
        strip = strip - jnp.dot(factor, factor[low:low + P_SIZE].T, precision=hi)
        if p == 1:
            strip = strip - jnp.dot(previous.T, previous[:, low:low + P_SIZE], precision=hi)
        strip = strip + ridge[0] * (ids[:, None] == low + local[None, :]).astype(jnp.float32)
        chol = jnp.linalg.cholesky(strip[low:low + P_SIZE])
        solved = lax.linalg.triangular_solve(chol, strip.T, left_side=True, lower=True)
        solved = jnp.where(ids[None, :] >= low + local[:, None], solved, 0.0)
        results.append(solved)
        previous = solved
    return jnp.stack(results)
```

```python
import jax
import jax.numpy as jnp
from jax import lax
from jax.experimental import pallas as pl
from jax.experimental.pallas import tpu as pltpu
from jax.sharding import PartitionSpec as P

HI = lax.Precision.HIGHEST
F32 = jnp.float32
B16 = jnp.bfloat16

def full(x):
    return jnp.broadcast_to(x, (8, 128))

def base(at, w, sub, lane):
    for k in range(16):
        lo = 8 * k
        tile = at[lo:lo + 8, :]
        cb = [full(tile[:, lo + j:lo + j + 1]) for j in range(8)]
        inblk = (lane >= lo) & (lane < lo + 8)
        rows = jnp.where(inblk, jnp.where(lane - lo == sub, 1.0, 0.0), tile)
        wc = [jnp.where(sub == j, 1.0, 0.0).astype(F32) for j in range(8)]
        piv = []
        diag = jnp.zeros((8, 128), F32)
        for j in range(8):
            d = full(cb[j][j:j + 1, :])
            p = 1.0 / d
            piv.append(p)
            diag = jnp.where(sub == j, d, diag)
            for jj in range(j + 1, 8):
                f = full(cb[j][jj:jj + 1, :]) * p
                cb[jj] = cb[jj] - cb[j] * f
            if j < 7:
                m = jnp.where(sub > j, cb[j] * p, 0.0)
                rows = rows - m * full(rows[j:j + 1, :])
                for jj in range(j + 1):
                    wc[jj] = wc[jj] - m * full(wc[jj][j:j + 1, :])
        w[lo:lo + 8, :] = jnp.where(lane <= lo + sub, rows, 0.0) * lax.rsqrt(diag)
        if k < 15:
            scaled = [full(rows[j:j + 1, :]) * piv[j] for j in range(8)]
            ys = []
            for j in range(8):
                y = scaled[j]
                for jj in range(j + 1, 8):
                    y = y + full(wc[j][jj:jj + 1, :]) * scaled[jj]
                ys.append(y)
            for t in range(k + 1, 16):
                old = at[8 * t:8 * t + 8, :]
                acc = jnp.where(inblk, 0.0, old)
                for j in range(8):
                    acc = acc - full(old[:, lo + j:lo + j + 1]) * ys[j]
                at[8 * t:8 * t + 8, :] = acc

def hdot(a, b, ca=1, cb=0):
    return lax.dot_general(a, b, (((ca,), (cb,)), ((), ())), precision=HI, preferred_element_type=F32)

def bdot(a, b, ca=1, cb=0):
    return lax.dot_general(a, b, (((ca,), (cb,)), ((), ())), preferred_element_type=F32)

def gram(g, lf, lr, aug, ridge):
    for q in range(4):
        cut = slice(128 * q, 128 * (q + 1))
        for c in range(8):
            lr[cut, 128 * c:128 * (c + 1)] = g[c // 2, c % 2, q, 128:256, :]
            f = jnp.maximum(g[c // 2, c % 2, q, 0:128, :], 0)
            lf[cut, 128 * c:128 * (c + 1)] = f.T
    for q in range(4):
        cut = slice(128 * q, 128 * (q + 1))
        a = lf[cut, :]
        r = lr[cut, :]
        s = bdot(a, lf[128 * q:512, :], 1, 1) * (1.0 / 1024) - bdot(r, lr[128 * q:512, :], 1, 1)
        row = lax.broadcasted_iota(jnp.int32, s.shape, 0)
        col = lax.broadcasted_iota(jnp.int32, s.shape, 1)
        aug[cut, 128 * q:512] = s + jnp.where(row == col, ridge, 0.0)

def strip(xf, xr, lf, lr, aug, ridge, first_col):
    f = jnp.maximum(xf[...], 0)
    s = bdot(lf[...], f) * (1.0 / 1024) - bdot(lr[...], xr[...], 1, 1)
    row = lax.broadcasted_iota(jnp.int32, s.shape, 0)
    col = lax.broadcasted_iota(jnp.int32, s.shape, 1) + first_col
    aug[:, 512:768] = s + jnp.where(row == col, ridge, 0.0)

def factor(q, at, w, aug, sub, lane):
    cut = pl.ds(pl.multiple_of(q * 128, 128), 128)
    at[...] = aug[cut, cut]
    base(at, w, sub, lane)

def outer(q, w, aug, out, first_col):
    cut = slice(128 * q, 128 * (q + 1))
    x = hdot(w[...], aug[cut, 128 * (q + 1):768])
    if q < 3:
        aug[cut, 128 * (q + 1):768] = x
        for i in range(q + 1, 4):
            left = aug[cut, 128 * i:128 * (i + 1)]
            rows = slice(128 * i, 128 * (i + 1))
            aug[rows, 128 * i:768] = aug[rows, 128 * i:768] - hdot(left, x[:, 128 * (i - q - 1):], 0, 0)
    mine = x[:, 128 * (3 - q):]
    row = lax.broadcasted_iota(jnp.int32, mine.shape, 0) + 128 * q
    col = lax.broadcasted_iota(jnp.int32, mine.shape, 1) + first_col
    out[...] = jnp.where(col >= row, mine, 0.0)


MESH = pl.DeviceIdType.MESH


def remote(src, dst, send, recv, row, col):
    return pltpu.make_async_remote_copy(
        src_ref=src, dst_ref=dst, send_sem=send, recv_sem=recv, device_id=(row, col), device_id_type=MESH
    )


def kernel(pre, res, rd, out, g, xf, xr, lf, lr, aug, at, w, fin, loc, s1, r1, s2, r2, s3, r3, s4, r4, s5, r5, s6, r6):
    row = lax.axis_index("row")
    col = lax.axis_index("col")
    zhi = lax.rem(row, 2)
    spot = row // 2
    zlo = col // 2
    core = lax.rem(col, 2)
    deep = zhi * 4 + zlo
    other = col + 1 - 2 * core
    ridge = rd[0]
    first_col = row * 2048 + col * 256
    sub = lax.broadcasted_iota(jnp.int32, (8, 128), 0)
    lane = lax.broadcasted_iota(jnp.int32, (8, 128), 1)

    def in_plane(d):
        return 2 * lax.rem(spot + d, 16) + zhi, col

    def in_ring(d):
        z = lax.rem(deep + d, 8)
        return 2 * spot + z // 4, 2 * lax.rem(z, 4) + core

    barrier = pltpu.get_barrier_semaphore()
    peers = [in_plane(d) for d in range(1, 16)] + [in_ring(d) for d in range(1, 8)]
    peers += [(row, 2 * z + 1 - core) for z in range(4)]
    for peer in peers:
        pl.semaphore_signal(barrier, inc=1, device_id=peer, device_id_type=MESH)
    pl.semaphore_wait(barrier, len(peers))

    def piece(q, p):
        if p < 8:
            return pre.at[16 * p:16 * p + 16, 128 * q:128 * q + 128]
        return res.at[128 * q + 16 * (p - 8):128 * q + 16 * (p - 8) + 16, :]

    def scatter(q, p):
        return remote(piece(q, p), g.at[zlo, core, q, 16 * p:16 * p + 16, :], s1.at[q, p], r1.at[q], 2 * p, col)

    def own(q):
        return pltpu.make_async_copy(piece(q, 0), g.at[zlo, core, q, 0:16, :], s1.at[q, 0])

    mine = pl.ds(pl.multiple_of(16 * spot, 16), 16)

    def along_ring(q, d):
        ref = g.at[zlo, core, q, mine, :]
        return remote(ref, ref, s2.at[q, d], r2.at[q, zlo], *in_ring(d))

    def ring_arrival(q, z):
        ref = g.at[z, core, q, mine, :]
        return remote(ref, ref, s2.at[q, 0], r2.at[q, z], row, col)

    def across(q, d):
        ref = g.at[:, core, q, mine, :]
        return remote(ref, ref, s3.at[q, d], r3.at[q, d], *in_plane(d))

    def to_partner(q):
        ref = g.at[:, core, q]
        return remote(ref, ref, s4.at[q], r4.at[q], row, other)

    root = (spot == 0) & (zhi == 0)

    @pl.when(root)
    def _():
        for q in range(4):
            own(q).start()
            for p in range(1, 16):
                scatter(q, p).start()

    for q in range(4):
        @pl.when(zhi == 0)
        def _():
            @pl.when(spot == 0)
            def _():
                own(q).wait()

            @pl.when(spot != 0)
            def _():
                scatter(q, 1).wait_recv()

            for d in range(1, 8):
                along_ring(q, d).start()

    for q in range(4):
        for z in range(4):
            @pl.when((zhi != 0) | (zlo != z))
            def _():
                ring_arrival(q, z).wait_recv()
        for d in range(1, 16):
            across(q, d).start()

    def move_cols(d):
        to = lax.rem(col + d, 8)
        return remote(
            pre.at[:, pl.ds(pl.multiple_of(256 * to, 256), 256)],
            xf.at[pl.ds(pl.multiple_of(128 * col, 128), 128), :], s5.at[0, d], r5.at[0, d], row, to)

    def move_rows(d):
        to = lax.rem(col + d, 8)
        return remote(
            res.at[pl.ds(pl.multiple_of(256 * to, 256), 256), :],
            xr.at[:, pl.ds(pl.multiple_of(128 * col, 128), 128)], s5.at[1, d], r5.at[1, d], row, to)

    keep_cols = pltpu.make_async_copy(
        pre.at[:, pl.ds(pl.multiple_of(256 * col, 256), 256)],
        xf.at[pl.ds(pl.multiple_of(128 * col, 128), 128), :], loc.at[0])
    keep_rows = pltpu.make_async_copy(
        res.at[pl.ds(pl.multiple_of(256 * col, 256), 256), :],
        xr.at[:, pl.ds(pl.multiple_of(128 * col, 128), 128)], loc.at[1])
    keep_cols.start()
    keep_rows.start()
    for d in range(1, 8):
        move_cols(d).start()
        move_rows(d).start()

    for q in range(4):
        for d in range(1, 16):
            across(q, d).wait_recv()
        to_partner(q).start()
    for q in range(4):
        to_partner(q).wait_recv()

    gram(g, lf, lr, aug, ridge)
    keep_cols.wait()
    keep_rows.wait()
    for d in range(1, 8):
        move_cols(d).wait_recv()
        move_rows(d).wait_recv()
    strip(xf, xr, lf, lr, aug, ridge, first_col)

    here = pl.ds(pl.multiple_of(256 * col, 256), 256)

    def deliver(q, i):
        to = 4 * (q % 2) + i
        return remote(
            fin.at[q, 32 * i:32 * i + 32, :], out.at[q // 2, :, here], s6.at[q, i], r6.at[q // 2, col], row, to)

    def keep(q, i):
        return pltpu.make_async_copy(fin.at[q, 32 * i:32 * i + 32, :], out.at[q // 2, :, here], s6.at[q, i])

    def turn(q, carry):
        factor(q, at, w, aug, sub, lane)
        for s in range(4):
            @pl.when(q == s)
            def _():
                outer(s, w, aug, fin.at[s], first_col)
                for i in range(4):
                    to = 4 * (s % 2) + i

                    @pl.when(col == to)
                    def _():
                        keep(s, i).start()

                    @pl.when(col != to)
                    def _():
                        deliver(s, i).start()
        return carry

    lax.fori_loop(0, 4, turn, 0)

    for half in range(2):
        for c in range(8):
            @pl.when(col != c)
            def _():
                ref = out.at[half, :, 256 * c:256 * c + 256]
                remote(fin.at[0, 0:32, :], ref, s6.at[0, 0], r6.at[half, c], row, col).wait_recv()

    for q in range(4):
        for i in range(4):
            to = 4 * (q % 2) + i

            @pl.when(col == to)
            def _():
                keep(q, i).wait()

            @pl.when(col != to)
            def _():
                deliver(q, i).wait_send()
    for d in range(1, 8):
        move_cols(d).wait_send()
        move_rows(d).wait_send()
    for q in range(4):
        to_partner(q).wait_send()
        for d in range(1, 16):
            across(q, d).wait_send()

        @pl.when(zhi == 0)
        def _():
            for d in range(1, 8):
                along_ring(q, d).wait_send()

    @pl.when(root)
    def _():
        for q in range(4):
            for p in range(1, 16):
                scatter(q, p).wait_send()


def local(preacts, resident, ridge):
    dma = pltpu.SemaphoreType.DMA
    return pl.pallas_call(
        kernel,
        out_shape=jax.ShapeDtypeStruct((2, 32, 2048), F32),
        in_specs=[
            pl.BlockSpec(memory_space=pl.ANY),
            pl.BlockSpec(memory_space=pl.ANY),
            pl.BlockSpec(memory_space=pltpu.SMEM),
        ],
        out_specs=pl.BlockSpec(memory_space=pl.ANY),
        scratch_shapes=[
            pltpu.VMEM((4, 2, 4, 256, 128), B16),
            pltpu.VMEM((1024, 256), B16),
            pltpu.VMEM((256, 1024), B16),
            pltpu.VMEM((512, 1024), B16),
            pltpu.VMEM((512, 1024), B16),
            pltpu.VMEM((512, 768), F32),
            pltpu.VMEM((128, 128), F32),
            pltpu.VMEM((128, 128), F32),
            pltpu.VMEM((4, 128, 256), F32),
            dma((2,)),
            dma((4, 16)), dma((4,)),
            dma((4, 8)), dma((4, 4)),
            dma((4, 16)), dma((4, 16)),
            dma((4,)), dma((4,)),
            dma((2, 8)), dma((2, 8)),
            dma((4, 4)), dma((2, 8)),
        ],
        compiler_params=pltpu.CompilerParams(collective_id=0, has_side_effects=True),
    )(preacts, resident, ridge)


def solution(mesh):
    placed = (P("col", "row"), P("row", "col"), P())
    return jax.shard_map(
        local, mesh=mesh, in_specs=placed, out_specs=P(None, "col", "row"), check_vma=False
    )
```

```python
import jax
import jax.numpy as jnp
from jax import lax
from jax.experimental import pallas as pl
from jax.experimental.pallas import tpu as pltpu
from jax.sharding import PartitionSpec as P

HI = lax.Precision.HIGHEST
F32 = jnp.float32
B16 = jnp.bfloat16

def full(x):
    return jnp.broadcast_to(x, (8, 128))

def row_of(x, j):
    return full(x[j:j + 1, :])


def columns(tile, lo):
    return [full(tile[:, lo + j:lo + j + 1]) for j in range(8)]


def base(at, w, sub, lane, hook=None):
    cb = columns(at[0:8, :], 0)
    for k in range(16):
        lo = 8 * k
        tile = at[lo:lo + 8, :]
        inblk = (lane >= lo) & (lane < lo + 8)
        rows = jnp.where(inblk, jnp.where(lane - lo == sub, 1.0, 0.0), tile)
        wc = [jnp.where(sub == j, 1.0, 0.0).astype(F32) for j in range(8)]
        if k < 15:
            below = at[lo + 8:lo + 16, :]
            first = columns(below, lo)
            nb = columns(below, lo + 8)
            c = list(first)
        piv = []
        diag = jnp.zeros((8, 128), F32)
        for j in range(8):
            d = row_of(cb[j], j)
            p = 1.0 / d
            piv.append(p)
            diag = jnp.where(sub == j, d, diag)
            u = [row_of(cb[j], jj) for jj in range(j + 1, 8)]
            for jj in range(j + 1, 8):
                cb[jj] = cb[jj] - (cb[j] * u[jj - j - 1]) * p
            if k < 15:
                m = c[j] * p
                for jj in range(j + 1, 8):
                    c[jj] = c[jj] - m * u[jj - j - 1]
                for jj in range(8):
                    nb[jj] = nb[jj] - m * row_of(c[j], jj)
            if j < 7:
                m = jnp.where(sub > j, cb[j] * p, 0.0)
                rows = rows - m * row_of(rows, j)
                for jj in range(j + 1):
                    wc[jj] = wc[jj] - m * row_of(wc[jj], j)
        w[lo:lo + 8, :] = jnp.where(lane <= lo + sub, rows, 0.0) * lax.rsqrt(diag)
        if k < 15:
            scaled = [row_of(rows, j) * piv[j] for j in range(8)]
            ys = []
            for j in range(8):
                y = scaled[j]
                for jj in range(j + 1, 8):
                    y = y + row_of(wc[j], jj) * scaled[jj]
                ys.append(y)
            for t in range(k + 1, 16):
                old = at[8 * t:8 * t + 8, :]
                cols = first if t == k + 1 else columns(old, lo)
                parts = [cols[j] * ys[j] for j in range(8)]
                while len(parts) > 1:
                    parts = [a + b for a, b in zip(parts[::2], parts[1::2])]
                at[8 * t:8 * t + 8, :] = jnp.where(inblk, 0.0, old) - parts[0]
            cb = nb
        if hook is not None and k % 4 == 3:
            hook(k // 4)


def hdot(a, b, ca=1, cb=0):
    return lax.dot_general(a, b, (((ca,), (cb,)), ((), ())), precision=HI, preferred_element_type=F32)

def bdot(a, b, ca=1, cb=0):
    return lax.dot_general(a, b, (((ca,), (cb,)), ((), ())), preferred_element_type=F32)

def load_chunk(s, g, lf, lr):
    cut = slice(128 * s, 128 * (s + 1))
    for c in range(8):
        lr[cut, 128 * c:128 * (c + 1)] = g[c // 2, c % 2, s, 128:256, :]
        f = jnp.maximum(g[c // 2, c % 2, s, 0:128, :], 0)
        lf[cut, 128 * c:128 * (c + 1)] = f.T


def diag_block(s, lf, lr, inv, tq, at, ridge):
    cut = slice(128 * s, 128 * (s + 1))
    top = slice(0, 128 * (s + 1))
    d = bdot(lf[top, :], lf[cut, :], 1, 1) * (1.0 / 1024) - bdot(lr[top, :], lr[cut, :], 1, 1)
    own = d[128 * s:, :]
    row = lax.broadcasted_iota(jnp.int32, own.shape, 0)
    col = lax.broadcasted_iota(jnp.int32, own.shape, 1)
    own = own + jnp.where(row == col, ridge, 0.0)
    if s > 0:
        lead = inv[0:128 * s, 0:128 * s]
        x = hdot(lead, d[:128 * s, :])
        own = own - hdot(x, x, 0, 0)
        tq[:, 0:128 * s] = hdot(x, lead, 0, 0)
    at[...] = own


def keep_inverse(s, w, tq, inv):
    cut = slice(128 * s, 128 * (s + 1))
    inv[cut, cut] = w[...]
    if 0 < s < 3:
        inv[cut, 0:128 * s] = -hdot(w[...], tq[:, 0:128 * s])


def strip(s, xf, xr, lf, lr, strips, ridge, first_col):
    cut = slice(128 * s, 128 * (s + 1))
    part = bdot(lf[cut, :], xf[...]) * (1.0 / 1024) - bdot(lr[cut, :], xr[...], 1, 1)
    row = lax.broadcasted_iota(jnp.int32, part.shape, 0) + 128 * s
    col = lax.broadcasted_iota(jnp.int32, part.shape, 1) + first_col
    strips[cut, :] = part + jnp.where(row == col, ridge, 0.0)


MESH = pl.DeviceIdType.MESH


def remote(src, dst, send, recv, row, col):
    return pltpu.make_async_remote_copy(
        src_ref=src, dst_ref=dst, send_sem=send, recv_sem=recv, device_id=(row, col), device_id_type=MESH
    )


def kernel(pre, res, rd, out, g, xf, xr, lf, lr, inv, tq, strips, left, at, w, fin, loc, s1, r1, s2, r2, s3, r3, s4, r4, s5, r5, s6, r6):
    row = lax.axis_index("row")
    col = lax.axis_index("col")
    zhi = lax.rem(row, 2)
    spot = row // 2
    zlo = col // 2
    core = lax.rem(col, 2)
    deep = zhi * 4 + zlo
    other = col + 1 - 2 * core
    ridge = rd[0]
    first_col = row * 2048 + col * 256
    sub = lax.broadcasted_iota(jnp.int32, (8, 128), 0)
    lane = lax.broadcasted_iota(jnp.int32, (8, 128), 1)

    def in_plane(d):
        return 2 * lax.rem(spot + d, 16) + zhi, col

    def in_ring(d):
        z = lax.rem(deep + d, 8)
        return 2 * spot + z // 4, 2 * lax.rem(z, 4) + core

    barrier = pltpu.get_barrier_semaphore()
    peers = [in_plane(d) for d in range(1, 16)] + [in_ring(d) for d in range(1, 8)]
    peers += [(row, 2 * z + 1 - core) for z in range(4)]
    for peer in peers:
        pl.semaphore_signal(barrier, inc=1, device_id=peer, device_id_type=MESH)
    pl.semaphore_wait(barrier, len(peers))

    def piece(q, p):
        if p < 8:
            return pre.at[16 * p:16 * p + 16, 128 * q:128 * q + 128]
        return res.at[128 * q + 16 * (p - 8):128 * q + 16 * (p - 8) + 16, :]

    def scatter(q, p):
        return remote(piece(q, p), g.at[zlo, core, q, 16 * p:16 * p + 16, :], s1.at[q, p], r1.at[q], 2 * p, col)

    def own(q):
        return pltpu.make_async_copy(piece(q, 0), g.at[zlo, core, q, 0:16, :], s1.at[q, 0])

    mine = pl.ds(pl.multiple_of(16 * spot, 16), 16)

    def along_ring(q, d):
        ref = g.at[zlo, core, q, mine, :]
        return remote(ref, ref, s2.at[q, d], r2.at[q, zlo], *in_ring(d))

    def ring_arrival(q, z):
        ref = g.at[z, core, q, mine, :]
        return remote(ref, ref, s2.at[q, 0], r2.at[q, z], row, col)

    def across(q, d):
        ref = g.at[:, core, q, mine, :]
        return remote(ref, ref, s3.at[q, d], r3.at[q, d], *in_plane(d))

    def to_partner(q):
        ref = g.at[:, core, q]
        return remote(ref, ref, s4.at[q], r4.at[q], row, other)

    root = (spot == 0) & (zhi == 0)

    def move_cols(d):
        to = lax.rem(col + d, 8)
        return remote(
            pre.at[:, pl.ds(pl.multiple_of(256 * to, 256), 256)],
            xf.at[pl.ds(pl.multiple_of(128 * col, 128), 128), :], s5.at[0, d], r5.at[0, d], row, to)

    def move_rows(d):
        to = lax.rem(col + d, 8)
        return remote(
            res.at[pl.ds(pl.multiple_of(256 * to, 256), 256), :],
            xr.at[:, pl.ds(pl.multiple_of(128 * col, 128), 128)], s5.at[1, d], r5.at[1, d], row, to)

    keep_cols = pltpu.make_async_copy(
        pre.at[:, pl.ds(pl.multiple_of(256 * col, 256), 256)],
        xf.at[pl.ds(pl.multiple_of(128 * col, 128), 128), :], loc.at[0])
    keep_rows = pltpu.make_async_copy(
        res.at[pl.ds(pl.multiple_of(256 * col, 256), 256), :],
        xr.at[:, pl.ds(pl.multiple_of(128 * col, 128), 128)], loc.at[1])
    here = pl.ds(pl.multiple_of(256 * col, 256), 256)

    def deliver(q, i):
        to = 4 * (q % 2) + i
        return remote(
            fin.at[q, 32 * i:32 * i + 32, :], out.at[q // 2, :, here], s6.at[q, i], r6.at[q // 2, col], row, to)

    def keep(q, i):
        return pltpu.make_async_copy(fin.at[q, 32 * i:32 * i + 32, :], out.at[q // 2, :, here], s6.at[q, i])

    def send_piece(q, i):
        to = 4 * lax.rem(q, 2) + i

        @pl.when(col == to)
        def _():
            keep(q, i).start()

        @pl.when(col != to)
        def _():
            deliver(q, i).start()

    @pl.when(root)
    def _():
        for q in range(4):
            own(q).start()
            for p in range(1, 16):
                scatter(q, p).start()

    keep_cols.start()
    keep_rows.start()
    for d in (1, 2, 6, 7):
        move_cols(d).start()
    inv[...] = jnp.zeros_like(inv)

    def forward_ring(q):
        @pl.when(zhi == 0)
        def _():
            @pl.when(spot == 0)
            def _():
                own(q).wait()

            @pl.when(spot != 0)
            def _():
                scatter(q, 1).wait_recv()

            for d in range(1, 8):
                along_ring(q, d).start()

    def forward_plane(q):
        for z in range(4):
            @pl.when((zhi != 0) | (zlo != z))
            def _():
                ring_arrival(q, z).wait_recv()
        for d in range(1, 16):
            across(q, d).start()

    def share(q):
        for d in range(1, 16):
            across(q, d).wait_recv()
        to_partner(q).start()

    forward_ring(0)
    forward_plane(0)
    for q in range(1, 4):
        forward_ring(q)
    for d in (3, 4, 5):
        move_cols(d).start()
    for d in range(1, 8):
        move_rows(d).start()
    for q in range(1, 4):
        forward_plane(q)
    share(0)

    def arrived():
        keep_cols.wait()
        keep_rows.wait()
        for d in range(1, 8):
            move_cols(d).wait_recv()
            move_rows(d).wait_recv()
        xf[...] = jnp.maximum(xf[...], 0)

    def hook(q, i):
        if i == 1:
            @pl.when(q < 3)
            def _():
                share(q + 1)

        @pl.when(q == 3)
        def _():
            fin[3, 32 * i:32 * i + 32, :] = hdot(w[32 * i:32 * i + 32, :], left[...])
            send_piece(3, i)

    def turn(q, carry):
        for s in range(4):
            @pl.when(q == s)
            def _():
                to_partner(s).wait_recv()
                load_chunk(s, g, lf, lr)
                diag_block(s, lf, lr, inv, tq, at, ridge)
                if s == 3:
                    strip(3, xf, xr, lf, lr, strips, ridge, first_col)
                    left[...] = strips[384:512, :] - hdot(tq[...], strips[0:384, :])
        base(at, w, sub, lane, lambda i: hook(q, i))
        for s in range(3):
            @pl.when(q == s)
            def _():
                keep_inverse(s, w, tq, inv)
                if s == 2:
                    arrived()
                    for e in range(3):
                        strip(e, xf, xr, lf, lr, strips, ridge, first_col)
                        top = 128 * (e + 1)
                        fin[e] = hdot(inv[128 * e:top, 0:top], strips[0:top, :])
                        for i in range(4):
                            send_piece(e, i)
        return carry

    lax.fori_loop(0, 4, turn, 0)

    for half in range(2):
        for c in range(8):
            @pl.when(col != c)
            def _():
                ref = out.at[half, :, 256 * c:256 * c + 256]
                remote(fin.at[0, 0:32, :], ref, s6.at[0, 0], r6.at[half, c], row, col).wait_recv()

    for q in range(4):
        for i in range(4):
            to = 4 * (q % 2) + i

            @pl.when(col == to)
            def _():
                keep(q, i).wait()

            @pl.when(col != to)
            def _():
                deliver(q, i).wait_send()
    for d in range(1, 8):
        move_cols(d).wait_send()
        move_rows(d).wait_send()
    for q in range(4):
        to_partner(q).wait_send()
        for d in range(1, 16):
            across(q, d).wait_send()

        @pl.when(zhi == 0)
        def _():
            for d in range(1, 8):
                along_ring(q, d).wait_send()

    @pl.when(root)
    def _():
        for q in range(4):
            for p in range(1, 16):
                scatter(q, p).wait_send()


def local(preacts, resident, ridge):
    dma = pltpu.SemaphoreType.DMA
    raw = pl.pallas_call(
        kernel,
        out_shape=jax.ShapeDtypeStruct((2, 32, 2048), F32),
        in_specs=[
            pl.BlockSpec(memory_space=pl.ANY),
            pl.BlockSpec(memory_space=pl.ANY),
            pl.BlockSpec(memory_space=pltpu.SMEM),
        ],
        out_specs=pl.BlockSpec(memory_space=pl.ANY),
        scratch_shapes=[
            pltpu.VMEM((4, 2, 4, 256, 128), B16),
            pltpu.VMEM((1024, 256), B16),
            pltpu.VMEM((256, 1024), B16),
            pltpu.VMEM((512, 1024), B16),
            pltpu.VMEM((512, 1024), B16),
            pltpu.VMEM((512, 512), F32),
            pltpu.VMEM((128, 384), F32),
            pltpu.VMEM((512, 256), F32),
            pltpu.VMEM((128, 256), F32),
            pltpu.VMEM((128, 128), F32),
            pltpu.VMEM((128, 128), F32),
            pltpu.VMEM((4, 128, 256), F32),
            dma((2,)),
            dma((4, 16)), dma((4,)),
            dma((4, 8)), dma((4, 4)),
            dma((4, 16)), dma((4, 16)),
            dma((4,)), dma((4,)),
            dma((2, 8)), dma((2, 8)),
            dma((4, 4)), dma((2, 8)),
        ],
        compiler_params=pltpu.CompilerParams(collective_id=0, has_side_effects=True),
    )(preacts, resident, ridge)
    column = lax.axis_index("row") * 2048 + lax.broadcasted_iota(jnp.int32, raw.shape, 2)
    line = lax.broadcasted_iota(jnp.int32, raw.shape, 0) * 256 + lax.broadcasted_iota(jnp.int32, raw.shape, 1)
    return jnp.where(column >= line + lax.axis_index("col") * 32, raw, 0.0)


def solution(mesh):
    placed = (P("col", "row"), P("row", "col"), P())
    return jax.shard_map(
        local, mesh=mesh, in_specs=placed, out_specs=P(None, "col", "row"), check_vma=False
    )
```

```python
import jax
import jax.numpy as jnp
from jax import lax
from jax.experimental import pallas as pl
from jax.experimental.pallas import tpu as pltpu
from jax.sharding import PartitionSpec as P

HI = lax.Precision.HIGHEST
F32 = jnp.float32
B16 = jnp.bfloat16

def full(x):
    return jnp.broadcast_to(x, (8, 128))

def row_of(x, j):
    return full(x[j:j + 1, :])


def columns(tile, lo):
    return [full(tile[:, lo + j:lo + j + 1]) for j in range(8)]


def base(at, w, sub, lane, hook=None):
    cb = columns(at[0:8, :], 0)
    for k in range(16):
        lo = 8 * k
        tile = at[lo:lo + 8, :]
        inblk = (lane >= lo) & (lane < lo + 8)
        rows = jnp.where(inblk, jnp.where(lane - lo == sub, 1.0, 0.0), tile)
        wc = [jnp.where(sub == j, 1.0, 0.0).astype(F32) for j in range(8)]
        if k < 15:
            below = at[lo + 8:lo + 16, :]
            first = columns(below, lo)
            nb = columns(below, lo + 8)
            c = list(first)
        piv = []
        diag = jnp.zeros((8, 128), F32)
        for j in range(8):
            d = row_of(cb[j], j)
            p = 1.0 / d
            piv.append(p)
            diag = jnp.where(sub == j, d, diag)
            u = [row_of(cb[j], jj) for jj in range(j + 1, 8)]
            for jj in range(j + 1, 8):
                cb[jj] = cb[jj] - (cb[j] * u[jj - j - 1]) * p
            if k < 15:
                m = c[j] * p
                for jj in range(j + 1, 8):
                    c[jj] = c[jj] - m * u[jj - j - 1]
                for jj in range(8):
                    nb[jj] = nb[jj] - m * row_of(c[j], jj)
            if j < 7:
                m = jnp.where(sub > j, cb[j] * p, 0.0)
                rows = rows - m * row_of(rows, j)
                for jj in range(j + 1):
                    wc[jj] = wc[jj] - m * row_of(wc[jj], j)
        w[lo:lo + 8, :] = jnp.where(lane <= lo + sub, rows, 0.0) * lax.rsqrt(diag)
        if k < 15:
            scaled = [row_of(rows, j) * piv[j] for j in range(8)]
            ys = []
            for j in range(8):
                y = scaled[j]
                for jj in range(j + 1, 8):
                    y = y + row_of(wc[j], jj) * scaled[jj]
                ys.append(y)
            for t in range(k + 1, 16):
                old = at[8 * t:8 * t + 8, :]
                cols = first if t == k + 1 else columns(old, lo)
                parts = [cols[j] * ys[j] for j in range(8)]
                while len(parts) > 1:
                    parts = [a + b for a, b in zip(parts[::2], parts[1::2])]
                at[8 * t:8 * t + 8, :] = jnp.where(inblk, 0.0, old) - parts[0]
            cb = nb
        if hook is not None and k % 4 == 3:
            hook(k // 4)


def hdot(a, b, ca=1, cb=0):
    return lax.dot_general(a, b, (((ca,), (cb,)), ((), ())), precision=HI, preferred_element_type=F32)

def bdot(a, b, ca=1, cb=0):
    return lax.dot_general(a, b, (((ca,), (cb,)), ((), ())), preferred_element_type=F32)

def load_chunk(s, g, lf, lr):
    cut = slice(128 * s, 128 * (s + 1))
    for c in range(8):
        lr[cut, 128 * c:128 * (c + 1)] = g[c // 2, c % 2, s, 128:256, :]
        f = jnp.maximum(g[c // 2, c % 2, s, 0:128, :], 0)
        lf[cut, 128 * c:128 * (c + 1)] = f.T


def gram(lf, lr, rows, cols):
    return bdot(lf[rows, :], lf[cols, :], 1, 1) * (1.0 / 1024) - bdot(lr[rows, :], lr[cols, :], 1, 1)


def ridged(x, first_row, first_col, ridge):
    row = lax.broadcasted_iota(jnp.int32, x.shape, 0) + first_row
    col = lax.broadcasted_iota(jnp.int32, x.shape, 1) + first_col
    return x + jnp.where(row == col, ridge, 0.0)


def half_block(g, core):
    total = jnp.zeros((128, 128), F32)
    rest = jnp.zeros((128, 128), F32)
    for z in range(4):
        f = jnp.maximum(g[z, core, 0, 0:128, :], 0)
        r = g[z, core, 0, 128:256, :]
        total = total + bdot(f, f, 0, 0)
        rest = rest + bdot(r, r, 1, 1)
    return total * (1.0 / 1024) - rest


def second_block(w, lf, lr, u01, at, ridge):
    d = gram(lf, lr, slice(0, 256), slice(128, 256))
    x = hdot(w[...], d[:128, :])
    u01[...] = x
    at[...] = ridged(d[128:, :], 0, 0, ridge) - hdot(x, x, 0, 0)


def panels(w0, w, lf, lr, xf, xr, u01, aug, at, fin, ridge, first_col):
    aug[:, 0:256] = ridged(gram(lf, lr, slice(0, 512), slice(256, 512)), 0, 256, ridge)
    part = bdot(lf[...], xf[...]) * (1.0 / 1024) - bdot(lr[...], xr[...], 1, 1)
    aug[:, 256:512] = ridged(part, 0, first_col, ridge)
    x0 = hdot(w0[...], aug[0:128, :])
    aug[0:128, :] = x0
    fin[0] = x0[:, 256:512]
    x1 = hdot(w[...], aug[128:256, :] - hdot(u01[...], x0, 0, 0))
    aug[128:256, :] = x1
    fin[1] = x1[:, 256:512]
    left = aug[0:256, 0:128]
    at[...] = aug[256:384, 0:128] - hdot(left, left, 0, 0)


def lower_panels(aug):
    aug[256:384, 128:512] = aug[256:384, 128:512] - hdot(aug[0:256, 0:128], aug[0:256, 128:512], 0, 0)
    aug[384:512, 128:512] = aug[384:512, 128:512] - hdot(aug[0:256, 128:256], aug[0:256, 128:512], 0, 0)


def last_panel(w, aug, at, left, fin):
    x = hdot(w[...], aug[256:384, 128:512])
    fin[2] = x[:, 128:384]
    u = x[:, 0:128]
    at[...] = aug[384:512, 128:256] - hdot(u, u, 0, 0)
    left[...] = aug[384:512, 256:512] - hdot(u, x[:, 128:384], 0, 0)


MESH = pl.DeviceIdType.MESH


def remote(src, dst, send, recv, row, col):
    return pltpu.make_async_remote_copy(
        src_ref=src, dst_ref=dst, send_sem=send, recv_sem=recv, device_id=(row, col), device_id_type=MESH
    )


def kernel(pre, res, rd, out, g, xf, xr, lf, lr, aug, u01, half, left, at, w0, w, fin, loc, s1, r1, s2, r2, s3, r3, s4, r4, s5, r5, s6, r6, s7):
    row = lax.axis_index("row")
    col = lax.axis_index("col")
    zhi = lax.rem(row, 2)
    spot = row // 2
    zlo = col // 2
    core = lax.rem(col, 2)
    deep = zhi * 4 + zlo
    other = col + 1 - 2 * core
    ridge = rd[0]
    first_col = row * 2048 + col * 256
    sub = lax.broadcasted_iota(jnp.int32, (8, 128), 0)
    lane = lax.broadcasted_iota(jnp.int32, (8, 128), 1)

    def in_plane(d):
        return 2 * lax.rem(spot + d, 16) + zhi, col

    def in_ring(d):
        z = lax.rem(deep + d, 8)
        return 2 * spot + z // 4, 2 * lax.rem(z, 4) + core

    barrier = pltpu.get_barrier_semaphore()
    peers = [in_plane(d) for d in range(1, 16)] + [in_ring(d) for d in range(1, 8)]
    peers += [(row, 2 * z + 1 - core) for z in range(4)]
    for peer in peers:
        pl.semaphore_signal(barrier, inc=1, device_id=peer, device_id_type=MESH)
    with jax.named_scope("a_barrier"):
        pl.semaphore_wait(barrier, len(peers))

    def piece(q, p):
        if p < 8:
            return pre.at[16 * p:16 * p + 16, 128 * q:128 * q + 128]
        return res.at[128 * q + 16 * (p - 8):128 * q + 16 * (p - 8) + 16, :]

    def scatter(q, p):
        return remote(piece(q, p), g.at[zlo, core, q, 16 * p:16 * p + 16, :], s1.at[q, p], r1.at[q], 2 * p, col)

    def own(q):
        return pltpu.make_async_copy(piece(q, 0), g.at[zlo, core, q, 0:16, :], s1.at[q, 0])

    mine = pl.ds(pl.multiple_of(16 * spot, 16), 16)

    def along_ring(q, d):
        ref = g.at[zlo, core, q, mine, :]
        return remote(ref, ref, s2.at[q, d], r2.at[q, zlo], *in_ring(d))

    def ring_arrival(q, z):
        ref = g.at[z, core, q, mine, :]
        return remote(ref, ref, s2.at[q, 0], r2.at[q, z], row, col)

    def across(q, d):
        ref = g.at[:, core, q, mine, :]
        return remote(ref, ref, s3.at[q, d], r3.at[q, d], *in_plane(d))

    def to_partner(q):
        ref = g.at[:, core, q]
        return remote(ref, ref, s4.at[q], r4.at[q], row, other)

    root = (spot == 0) & (zhi == 0)

    def move_cols(d):
        to = lax.rem(col + d, 8)
        return remote(
            pre.at[:, pl.ds(pl.multiple_of(256 * to, 256), 256)],
            xf.at[pl.ds(pl.multiple_of(128 * col, 128), 128), :], s5.at[0, d], r5.at[0, d], row, to)

    def move_rows(d):
        to = lax.rem(col + d, 8)
        return remote(
            res.at[pl.ds(pl.multiple_of(256 * to, 256), 256), :],
            xr.at[:, pl.ds(pl.multiple_of(128 * col, 128), 128)], s5.at[1, d], r5.at[1, d], row, to)

    keep_cols = pltpu.make_async_copy(
        pre.at[:, pl.ds(pl.multiple_of(256 * col, 256), 256)],
        xf.at[pl.ds(pl.multiple_of(128 * col, 128), 128), :], loc.at[0])
    keep_rows = pltpu.make_async_copy(
        res.at[pl.ds(pl.multiple_of(256 * col, 256), 256), :],
        xr.at[:, pl.ds(pl.multiple_of(128 * col, 128), 128)], loc.at[1])
    here = pl.ds(pl.multiple_of(256 * col, 256), 256)

    def deliver(q, i):
        to = 4 * (q % 2) + i
        return remote(
            fin.at[q, 32 * i:32 * i + 32, :], out.at[q // 2, :, here], s6.at[q, i], r6.at[q // 2, col], row, to)

    def keep(q, i):
        return pltpu.make_async_copy(fin.at[q, 32 * i:32 * i + 32, :], out.at[q // 2, :, here], s6.at[q, i])

    def send_piece(q, i):
        to = 4 * lax.rem(q, 2) + i

        @pl.when(col == to)
        def _():
            keep(q, i).start()

        @pl.when(col != to)
        def _():
            deliver(q, i).start()

    @pl.when(root)
    def _():
        for q in range(4):
            own(q).start()
            for p in range(1, 16):
                scatter(q, p).start()

    keep_cols.start()
    keep_rows.start()
    for d in (1, 2, 6, 7):
        move_cols(d).start()

    def forward_ring(q):
        @pl.when(zhi == 0)
        def _():
            @pl.when(spot == 0)
            def _():
                own(q).wait()

            @pl.when(spot != 0)
            def _():
                scatter(q, 1).wait_recv()

            for d in range(1, 8):
                along_ring(q, d).start()

    def forward_plane(q):
        for z in range(4):
            @pl.when((zhi != 0) | (zlo != z))
            def _():
                ring_arrival(q, z).wait_recv()
        for d in range(1, 16):
            across(q, d).start()

    def swap():
        return remote(half.at[0], half.at[1], s7.at[0], s7.at[1], row, other)

    def gathered(q):
        for d in range(1, 16):
            across(q, d).wait_recv()

    def share(q):
        gathered(q)
        to_partner(q).start()

    with jax.named_scope("b_ring0"):
        forward_ring(0)
    with jax.named_scope("c_plane0"):
        forward_plane(0)
    with jax.named_scope("d_ring123"):
        for q in range(1, 4):
            forward_ring(q)
    for d in (3, 4, 5):
        move_cols(d).start()
    for d in range(1, 8):
        move_rows(d).start()
    with jax.named_scope("e_plane123"):
        for q in range(1, 4):
            forward_plane(q)
    with jax.named_scope("f_gathered0"):
        gathered(0)

    def arrived():
        keep_cols.wait()
        keep_rows.wait()
        for d in range(1, 8):
            move_cols(d).wait_recv()
            move_rows(d).wait_recv()
        xf[...] = jnp.maximum(xf[...], 0)

    def hook(q, i):
        if i == 1:
            @pl.when(q < 2)
            def _():
                with jax.named_scope("j_share"):
                    share(q + 1)

        @pl.when(q == 3)
        def _():
            fin[3, 32 * i:32 * i + 32, :] = hdot(w[32 * i:32 * i + 32, :], left[...])
            send_piece(3, i)

    def turn(q, carry):
        with jax.named_scope("i_base"):
            base(at, w, sub, lane, lambda i: hook(q, i))

        @pl.when(q == 0)
        def _():
            w0[...] = w[...]
            with jax.named_scope("k_chunk01"):
                for s in range(2):
                    to_partner(s).wait_recv()
                    load_chunk(s, g, lf, lr)
            with jax.named_scope("k_second"):
                second_block(w, lf, lr, u01, at, ridge)

        @pl.when(q == 1)
        def _():
            with jax.named_scope("l_chunk23"):
                share(3)
                for s in range(2, 4):
                    to_partner(s).wait_recv()
                    load_chunk(s, g, lf, lr)
            with jax.named_scope("l_arrived"):
                arrived()
            with jax.named_scope("l_panels"):
                panels(w0, w, lf, lr, xf, xr, u01, aug, at, fin, ridge, first_col)
            for e in range(2):
                for i in range(4):
                    send_piece(e, i)
            with jax.named_scope("l_lower"):
                lower_panels(aug)

        @pl.when(q == 2)
        def _():
            with jax.named_scope("m_last"):
                last_panel(w, aug, at, left, fin)
            for i in range(4):
                send_piece(2, i)

        return carry

    with jax.named_scope("g_half"):
        half[0] = half_block(g, core)
    swap().start()
    to_partner(0).start()
    with jax.named_scope("h_swap"):
        swap().wait_recv()
    at[...] = ridged(half[0] + half[1], 0, 0, ridge)
    lax.fori_loop(0, 4, turn, 0)

    with jax.named_scope("n_final"):
        for p in range(2):
            for c in range(8):
                @pl.when(col != c)
                def _():
                    ref = out.at[p, :, 256 * c:256 * c + 256]
                    remote(fin.at[0, 0:32, :], ref, s6.at[0, 0], r6.at[p, c], row, col).wait_recv()

    for q in range(4):
        for i in range(4):
            to = 4 * (q % 2) + i

            @pl.when(col == to)
            def _():
                keep(q, i).wait()

            @pl.when(col != to)
            def _():
                deliver(q, i).wait_send()
    for d in range(1, 8):
        move_cols(d).wait_send()
        move_rows(d).wait_send()
    swap().wait_send()
    for q in range(4):
        to_partner(q).wait_send()
        for d in range(1, 16):
            across(q, d).wait_send()

        @pl.when(zhi == 0)
        def _():
            for d in range(1, 8):
                along_ring(q, d).wait_send()

    @pl.when(root)
    def _():
        for q in range(4):
            for p in range(1, 16):
                scatter(q, p).wait_send()


def local(preacts, resident, ridge):
    dma = pltpu.SemaphoreType.DMA
    raw = pl.pallas_call(
        kernel,
        out_shape=jax.ShapeDtypeStruct((2, 32, 2048), F32),
        in_specs=[
            pl.BlockSpec(memory_space=pl.ANY),
            pl.BlockSpec(memory_space=pl.ANY),
            pl.BlockSpec(memory_space=pltpu.SMEM),
        ],
        out_specs=pl.BlockSpec(memory_space=pl.ANY),
        scratch_shapes=[
            pltpu.VMEM((4, 2, 4, 256, 128), B16),
            pltpu.VMEM((1024, 256), B16),
            pltpu.VMEM((256, 1024), B16),
            pltpu.VMEM((512, 1024), B16),
            pltpu.VMEM((512, 1024), B16),
            pltpu.VMEM((512, 512), F32),
            pltpu.VMEM((128, 128), F32),
            pltpu.VMEM((2, 128, 128), F32),
            pltpu.VMEM((128, 256), F32),
            pltpu.VMEM((128, 128), F32),
            pltpu.VMEM((128, 128), F32),
            pltpu.VMEM((128, 128), F32),
            pltpu.VMEM((4, 128, 256), F32),
            dma((2,)),
            dma((4, 16)), dma((4,)),
            dma((4, 8)), dma((4, 4)),
            dma((4, 16)), dma((4, 16)),
            dma((4,)), dma((4,)),
            dma((2, 8)), dma((2, 8)),
            dma((4, 4)), dma((2, 8)),
            dma((2,)),
        ],
        compiler_params=pltpu.CompilerParams(collective_id=0, has_side_effects=True),
    )(preacts, resident, ridge)
    column = lax.axis_index("row") * 2048 + lax.broadcasted_iota(jnp.int32, raw.shape, 2)
    line = lax.broadcasted_iota(jnp.int32, raw.shape, 0) * 256 + lax.broadcasted_iota(jnp.int32, raw.shape, 1)
    return jnp.where(column >= line + lax.axis_index("col") * 32, raw, 0.0)


def solution(mesh):
    placed = (P("col", "row"), P("row", "col"), P())
    return jax.shard_map(
        local, mesh=mesh, in_specs=placed, out_specs=P(None, "col", "row"), check_vma=False
    )
```

```python
import jax
import jax.numpy as jnp
from jax import lax
from jax.experimental import pallas as pl
from jax.experimental.pallas import tpu as pltpu
from jax.sharding import PartitionSpec as P

HI = lax.Precision.HIGHEST
F32 = jnp.float32
B16 = jnp.bfloat16

def full(x):
    return jnp.broadcast_to(x, (8, 128))

def row_of(x, j):
    return full(x[j:j + 1, :])


def columns(tile, lo):
    return [full(tile[:, lo + j:lo + j + 1]) for j in range(8)]


def base(at, w, sub, lane, hook=None):
    cb = columns(at[0:8, :], 0)
    for k in range(16):
        lo = 8 * k
        tile = at[lo:lo + 8, :]
        inblk = (lane >= lo) & (lane < lo + 8)
        rows = jnp.where(inblk, jnp.where(lane - lo == sub, 1.0, 0.0), tile)
        wc = [jnp.where(sub == j, 1.0, 0.0).astype(F32) for j in range(8)]
        if k < 15:
            below = at[lo + 8:lo + 16, :]
            first = columns(below, lo)
            nb = columns(below, lo + 8)
            c = list(first)
        piv = []
        diag = jnp.zeros((8, 128), F32)
        for j in range(8):
            d = row_of(cb[j], j)
            p = 1.0 / d
            piv.append(p)
            diag = jnp.where(sub == j, d, diag)
            u = [row_of(cb[j], jj) for jj in range(j + 1, 8)]
            for jj in range(j + 1, 8):
                cb[jj] = cb[jj] - (cb[j] * u[jj - j - 1]) * p
            if k < 15:
                m = c[j] * p
                for jj in range(j + 1, 8):
                    c[jj] = c[jj] - m * u[jj - j - 1]
                for jj in range(8):
                    nb[jj] = nb[jj] - m * row_of(c[j], jj)
            if j < 7:
                m = jnp.where(sub > j, cb[j] * p, 0.0)
                rows = rows - m * row_of(rows, j)
                for jj in range(j + 1):
                    wc[jj] = wc[jj] - m * row_of(wc[jj], j)
        w[lo:lo + 8, :] = jnp.where(lane <= lo + sub, rows, 0.0) * lax.rsqrt(diag)
        if k < 15:
            scaled = [row_of(rows, j) * piv[j] for j in range(8)]
            ys = []
            for j in range(8):
                y = scaled[j]
                for jj in range(j + 1, 8):
                    y = y + row_of(wc[j], jj) * scaled[jj]
                ys.append(y)
            for t in range(k + 1, 16):
                old = at[8 * t:8 * t + 8, :]
                cols = first if t == k + 1 else columns(old, lo)
                parts = [cols[j] * ys[j] for j in range(8)]
                while len(parts) > 1:
                    parts = [a + b for a, b in zip(parts[::2], parts[1::2])]
                at[8 * t:8 * t + 8, :] = jnp.where(inblk, 0.0, old) - parts[0]
            cb = nb
        if hook is not None and k % 4 == 3:
            hook(k // 4)


def hdot(a, b, ca=1, cb=0):
    return lax.dot_general(a, b, (((ca,), (cb,)), ((), ())), precision=HI, preferred_element_type=F32)

def bdot(a, b, ca=1, cb=0):
    return lax.dot_general(a, b, (((ca,), (cb,)), ((), ())), preferred_element_type=F32)

def load_chunk(s, g, lf, lr):
    cut = slice(128 * s, 128 * (s + 1))
    for c in range(8):
        lr[cut, 128 * c:128 * (c + 1)] = g[c // 2, c % 2, s, 128:256, :]
        f = jnp.maximum(g[c // 2, c % 2, s, 0:128, :], 0)
        lf[cut, 128 * c:128 * (c + 1)] = f.T


def gram(lf, lr, rows, cols):
    return bdot(lf[rows, :], lf[cols, :], 1, 1) * (1.0 / 1024) - bdot(lr[rows, :], lr[cols, :], 1, 1)


def ridged(x, first_row, first_col, ridge):
    row = lax.broadcasted_iota(jnp.int32, x.shape, 0) + first_row
    col = lax.broadcasted_iota(jnp.int32, x.shape, 1) + first_col
    return x + jnp.where(row == col, ridge, 0.0)


def half_block(g, core):
    total = jnp.zeros((128, 128), F32)
    rest = jnp.zeros((128, 128), F32)
    for z in range(4):
        f = jnp.maximum(g[z, core, 0, 0:128, :], 0)
        r = g[z, core, 0, 128:256, :]
        total = total + bdot(f, f, 0, 0)
        rest = rest + bdot(r, r, 1, 1)
    return total * (1.0 / 1024) - rest


def second_block(w, lf, lr, u01, at, ridge):
    d = gram(lf, lr, slice(0, 256), slice(128, 256))
    x = hdot(w[...], d[:128, :])
    u01[...] = x
    at[...] = ridged(d[128:, :], 0, 0, ridge) - hdot(x, x, 0, 0)


def first_panels(cols, w0, w, u01, aug):
    x0 = hdot(w0[...], aug[0:128, cols])
    x1 = hdot(w[...], aug[128:256, cols] - hdot(u01[...], x0, 0, 0))
    aug[0:128, cols] = x0
    aug[128:256, cols] = x1
    return x0, x1


def strip(h, w0, w, u01, lf, lr, xf, xr, aug, fin, ridge, first_col):
    cut = slice(128 * h, 128 * h + 128)
    cols = slice(256 + 128 * h, 384 + 128 * h)
    f = jnp.maximum(xf[:, cut], 0)
    part = bdot(lf[...], f) * (1.0 / 1024) - bdot(lr[...], xr[cut, :], 1, 1)
    aug[:, cols] = ridged(part, 0, first_col + 128 * h, ridge)
    x0, x1 = first_panels(cols, w0, w, u01, aug)
    fin[0, :, cut] = x0
    fin[1, :, cut] = x1


def third_block(w0, w, u01, lf, lr, aug, at, ridge):
    cols = slice(0, 256)
    aug[:, cols] = ridged(gram(lf, lr, slice(0, 512), slice(256, 512)), 0, 256, ridge)
    first_panels(cols, w0, w, u01, aug)
    left = aug[0:256, 0:128]
    at[...] = aug[256:384, 0:128] - hdot(left, left, 0, 0)


def lower_panels(aug):
    aug[256:384, 128:512] = aug[256:384, 128:512] - hdot(aug[0:256, 0:128], aug[0:256, 128:512], 0, 0)
    aug[384:512, 128:512] = aug[384:512, 128:512] - hdot(aug[0:256, 128:256], aug[0:256, 128:512], 0, 0)


def last_panel(w, aug, at, left, fin):
    x = hdot(w[...], aug[256:384, 128:512])
    fin[2] = x[:, 128:384]
    u = x[:, 0:128]
    at[...] = aug[384:512, 128:256] - hdot(u, u, 0, 0)
    left[...] = aug[384:512, 256:512] - hdot(u, x[:, 128:384], 0, 0)


MESH = pl.DeviceIdType.MESH


def remote(src, dst, send, recv, row, col):
    return pltpu.make_async_remote_copy(
        src_ref=src, dst_ref=dst, send_sem=send, recv_sem=recv, device_id=(row, col), device_id_type=MESH
    )


def kernel(pre, res, rd, out, g, xf, xr, lf, lr, aug, u01, half, left, at, w0, w1, w, fin, s1, r1, s2, r2, s3, r3, s4, r4, s5, r5, s6, r6, s7):
    row = lax.axis_index("row")
    col = lax.axis_index("col")
    zhi = lax.rem(row, 2)
    spot = row // 2
    zlo = col // 2
    core = lax.rem(col, 2)
    deep = zhi * 4 + zlo
    other = col + 1 - 2 * core
    ridge = rd[0]
    first_col = row * 2048 + col * 256
    sub = lax.broadcasted_iota(jnp.int32, (8, 128), 0)
    lane = lax.broadcasted_iota(jnp.int32, (8, 128), 1)

    def in_plane(d):
        return 2 * lax.rem(spot + d, 16) + zhi, col

    def in_ring(d):
        z = lax.rem(deep + d, 8)
        return 2 * spot + z // 4, 2 * lax.rem(z, 4) + core

    barrier = pltpu.get_barrier_semaphore()
    peers = [in_plane(d) for d in range(1, 16)] + [in_ring(d) for d in range(1, 8)]
    peers += [(row, 2 * z + 1 - core) for z in range(4)]
    for peer in peers:
        pl.semaphore_signal(barrier, inc=1, device_id=peer, device_id_type=MESH)
    with jax.named_scope("a_barrier"):
        pl.semaphore_wait(barrier, len(peers))

    def piece(q, p):
        if p < 8:
            return pre.at[16 * p:16 * p + 16, 128 * q:128 * q + 128]
        return res.at[128 * q + 16 * (p - 8):128 * q + 16 * (p - 8) + 16, :]

    def scatter(q, p):
        return remote(piece(q, p), g.at[zlo, core, q, 16 * p:16 * p + 16, :], s1.at[q, p], r1.at[q], 2 * p, col)

    def own(q):
        return pltpu.make_async_copy(piece(q, 0), g.at[zlo, core, q, 0:16, :], s1.at[q, 0])

    mine = pl.ds(pl.multiple_of(16 * spot, 16), 16)

    def along_ring(q, d):
        ref = g.at[zlo, core, q, mine, :]
        return remote(ref, ref, s2.at[q, d], r2.at[q, zlo], *in_ring(d))

    def ring_arrival(q, z):
        ref = g.at[z, core, q, mine, :]
        return remote(ref, ref, s2.at[q, 0], r2.at[q, z], row, col)

    def across(q, d):
        ref = g.at[:, core, q, mine, :]
        return remote(ref, ref, s3.at[q, d], r3.at[q, d], *in_plane(d))

    def to_partner(q):
        ref = g.at[:, core, q]
        return remote(ref, ref, s4.at[q], r4.at[q], row, other)

    root = (spot == 0) & (zhi == 0)

    def block_of(to, h):
        return pl.ds(pl.multiple_of(256 * to + 128 * h, 128), 128)

    home = pl.ds(pl.multiple_of(128 * col, 128), 128)

    def places(h):
        cut = slice(128 * h, 128 * h + 128)
        return xf.at[home, cut], xr.at[cut, home]

    def move_cols(h, d):
        to = lax.rem(col + d, 8)
        return remote(pre.at[:, block_of(to, h)], places(h)[0], s5.at[2 * h, d], r5.at[2 * h, d], row, to)

    def move_rows(h, d):
        to = lax.rem(col + d, 8)
        return remote(res.at[block_of(to, h), :], places(h)[1], s5.at[2 * h + 1, d], r5.at[2 * h + 1, d], row, to)

    def stay(h):
        return [
            pltpu.make_async_copy(pre.at[:, block_of(col, h)], places(h)[0], s5.at[2 * h, 0]),
            pltpu.make_async_copy(res.at[block_of(col, h), :], places(h)[1], s5.at[2 * h + 1, 0]),
        ]

    here = pl.ds(pl.multiple_of(256 * col, 256), 256)

    def deliver(q, i):
        to = 4 * lax.rem(q, 2) + i
        return remote(
            fin.at[q, 32 * i:32 * i + 32, :], out.at[q // 2, :, here], s6.at[q, i], r6.at[q // 2, col], row, to)

    def deliver_half(q, i, h):
        to = 4 * lax.rem(q, 2) + i
        cut = slice(128 * h, 128 * h + 128)
        lanes = pl.ds(pl.multiple_of(256 * col + 128 * h, 128), 128)
        return remote(
            fin.at[q, 32 * i:32 * i + 32, cut], out.at[q // 2, :, lanes], s6.at[q, i], r6.at[q // 2, col], row, to)

    def keep(q, i):
        return pltpu.make_async_copy(fin.at[q, 32 * i:32 * i + 32, :], out.at[q // 2, :, here], s6.at[q, i])

    def send_piece(q, i):
        to = 4 * lax.rem(q, 2) + i

        @pl.when(col == to)
        def _():
            keep(q, i).start()

        @pl.when(col != to)
        def _():
            deliver(q, i).start()

    def send_half(q, i, h):
        to = 4 * lax.rem(q, 2) + i

        @pl.when(col != to)
        def _():
            deliver_half(q, i, h).start()

        if h == 1:
            @pl.when(col == to)
            def _():
                keep(q, i).start()

    @pl.when(root)
    def _():
        for q in range(4):
            own(q).start()
            for p in range(1, 16):
                scatter(q, p).start()

    for h in range(2):
        for copy in stay(h):
            copy.start()

    def move(kind, h, offsets):
        for d in offsets:
            kind(h, d).start()

    move(move_cols, 0, (1, 2, 6, 7))

    def forward_ring(q):
        @pl.when(zhi == 0)
        def _():
            @pl.when(spot == 0)
            def _():
                own(q).wait()

            @pl.when(spot != 0)
            def _():
                scatter(q, 1).wait_recv()

            for d in range(1, 8):
                along_ring(q, d).start()

    def forward_plane(q):
        for z in range(4):
            @pl.when((zhi != 0) | (zlo != z))
            def _():
                ring_arrival(q, z).wait_recv()
        for d in range(1, 16):
            across(q, d).start()

    def swap():
        return remote(half.at[0], half.at[1], s7.at[0], s7.at[1], row, other)

    def gathered(q):
        for d in range(1, 16):
            across(q, d).wait_recv()

    def share(q):
        gathered(q)
        to_partner(q).start()

    with jax.named_scope("b_ring0"):
        forward_ring(0)
    move(move_cols, 0, (3, 4, 5))
    with jax.named_scope("c_plane0"):
        forward_plane(0)
    with jax.named_scope("d_ring123"):
        for q in range(1, 4):
            forward_ring(q)
    move(move_rows, 0, range(1, 8))
    move(move_cols, 1, range(1, 8))
    move(move_rows, 1, range(1, 8))
    with jax.named_scope("e_plane123"):
        for q in range(1, 4):
            forward_plane(q)
    with jax.named_scope("f_gathered0"):
        gathered(0)

    def arrived(h):
        for copy in stay(h):
            copy.wait()
        for d in range(1, 8):
            move_cols(h, d).wait_recv()
            move_rows(h, d).wait_recv()

    def solve_half(h):
        with jax.named_scope("s_arrived"):
            arrived(h)
        with jax.named_scope("s_strip"):
            strip(h, w0, w1, u01, lf, lr, xf, xr, aug, fin, ridge, first_col)
        for e in range(2):
            for i in range(4):
                send_half(e, i, h)

    def hook(q, i):
        if i == 1:
            @pl.when(q < 2)
            def _():
                with jax.named_scope("j_share"):
                    share(q + 1)
        if i == 2:
            @pl.when(q == 1)
            def _():
                with jax.named_scope("j_share"):
                    share(3)
        if i == 0:
            @pl.when(q == 2)
            def _():
                solve_half(1)
                with jax.named_scope("s_lower"):
                    lower_panels(aug)

        @pl.when(q == 3)
        def _():
            fin[3, 32 * i:32 * i + 32, :] = hdot(w[32 * i:32 * i + 32, :], left[...])
            send_piece(3, i)

    def turn(q, carry):
        with jax.named_scope("i_base"):
            base(at, w, sub, lane, lambda i: hook(q, i))

        @pl.when(q == 0)
        def _():
            w0[...] = w[...]
            with jax.named_scope("k_chunk01"):
                for s in range(2):
                    to_partner(s).wait_recv()
                    load_chunk(s, g, lf, lr)
            with jax.named_scope("k_second"):
                second_block(w, lf, lr, u01, at, ridge)

        @pl.when(q == 1)
        def _():
            w1[...] = w[...]
            with jax.named_scope("l_chunk23"):
                for s in range(2, 4):
                    to_partner(s).wait_recv()
                    load_chunk(s, g, lf, lr)
            solve_half(0)
            with jax.named_scope("l_third"):
                third_block(w0, w1, u01, lf, lr, aug, at, ridge)

        @pl.when(q == 2)
        def _():
            with jax.named_scope("m_last"):
                last_panel(w, aug, at, left, fin)
            for i in range(4):
                send_piece(2, i)

        return carry

    with jax.named_scope("g_half"):
        half[0] = half_block(g, core)
    swap().start()
    to_partner(0).start()
    with jax.named_scope("h_swap"):
        swap().wait_recv()
    at[...] = ridged(half[0] + half[1], 0, 0, ridge)
    lax.fori_loop(0, 4, turn, 0)

    with jax.named_scope("n_final"):
        for p in range(2):
            for c in range(8):
                @pl.when(col != c)
                def _():
                    ref = out.at[p, :, 256 * c:256 * c + 256]
                    remote(fin.at[0, 0:32, :], ref, s6.at[0, 0], r6.at[p, c], row, col).wait_recv()

    for q in range(4):
        for i in range(4):
            to = 4 * (q % 2) + i

            @pl.when(col == to)
            def _():
                keep(q, i).wait()

            @pl.when(col != to)
            def _():
                deliver(q, i).wait_send()
    for h in range(2):
        for d in range(1, 8):
            move_cols(h, d).wait_send()
            move_rows(h, d).wait_send()
    swap().wait_send()
    for q in range(4):
        to_partner(q).wait_send()
        for d in range(1, 16):
            across(q, d).wait_send()

        @pl.when(zhi == 0)
        def _():
            for d in range(1, 8):
                along_ring(q, d).wait_send()

    @pl.when(root)
    def _():
        for q in range(4):
            for p in range(1, 16):
                scatter(q, p).wait_send()


def local(preacts, resident, ridge):
    dma = pltpu.SemaphoreType.DMA
    raw = pl.pallas_call(
        kernel,
        out_shape=pltpu.VMEM((2, 32, 2048), F32),
        in_specs=[
            pl.BlockSpec(memory_space=pl.ANY),
            pl.BlockSpec(memory_space=pl.ANY),
            pl.BlockSpec(memory_space=pltpu.SMEM),
        ],
        out_specs=pl.BlockSpec(memory_space=pltpu.VMEM),
        scratch_shapes=[
            pltpu.VMEM((4, 2, 4, 256, 128), B16),
            pltpu.VMEM((1024, 256), B16),
            pltpu.VMEM((256, 1024), B16),
            pltpu.VMEM((512, 1024), B16),
            pltpu.VMEM((512, 1024), B16),
            pltpu.VMEM((512, 512), F32),
            pltpu.VMEM((128, 128), F32),
            pltpu.VMEM((2, 128, 128), F32),
            pltpu.VMEM((128, 256), F32),
            pltpu.VMEM((128, 128), F32),
            pltpu.VMEM((128, 128), F32),
            pltpu.VMEM((128, 128), F32),
            pltpu.VMEM((128, 128), F32),
            pltpu.VMEM((4, 128, 256), F32),
            dma((4, 16)), dma((4,)),
            dma((4, 8)), dma((4, 4)),
            dma((4, 16)), dma((4, 16)),
            dma((4,)), dma((4,)),
            dma((4, 8)), dma((4, 8)),
            dma((4, 4)), dma((2, 8)),
            dma((2,)),
        ],
        compiler_params=pltpu.CompilerParams(collective_id=0, has_side_effects=True),
    )(preacts, resident, ridge)
    column = lax.axis_index("row") * 2048 + lax.broadcasted_iota(jnp.int32, raw.shape, 2)
    line = lax.broadcasted_iota(jnp.int32, raw.shape, 0) * 256 + lax.broadcasted_iota(jnp.int32, raw.shape, 1)
    return jnp.where(column >= line + lax.axis_index("col") * 32, raw, 0.0)


def solution(mesh):
    placed = (P("col", "row"), P("row", "col"), P())
    return jax.shard_map(
        local, mesh=mesh, in_specs=placed, out_specs=P(None, "col", "row"), check_vma=False
    )
```

```python
import jax
import jax.numpy as jnp
from jax import lax
from jax.experimental import pallas as pl
from jax.experimental.pallas import tpu as pltpu
from jax.sharding import PartitionSpec as P

HI = lax.Precision.HIGHEST
F32 = jnp.float32
B16 = jnp.bfloat16

def full(x):
    return jnp.broadcast_to(x, (8, 128))

def row_of(x, j):
    return full(x[j:j + 1, :])


def columns(tile, lo):
    return [full(tile[:, lo + j:lo + j + 1]) for j in range(8)]


def base(at, w, sub, lane, hook=None):
    cb = columns(at[0:8, :], 0)
    for k in range(16):
        lo = 8 * k
        tile = at[lo:lo + 8, :]
        inblk = (lane >= lo) & (lane < lo + 8)
        rows = jnp.where(inblk, jnp.where(lane - lo == sub, 1.0, 0.0), tile)
        wc = [jnp.where(sub == j, 1.0, 0.0).astype(F32) for j in range(8)]
        if k < 15:
            below = at[lo + 8:lo + 16, :]
            first = columns(below, lo)
            nb = columns(below, lo + 8)
            c = list(first)
        piv = []
        diag = jnp.zeros((8, 128), F32)
        for j in range(8):
            d = row_of(cb[j], j)
            p = 1.0 / d
            piv.append(p)
            diag = jnp.where(sub == j, d, diag)
            u = [row_of(cb[j], jj) for jj in range(j + 1, 8)]
            for jj in range(j + 1, 8):
                cb[jj] = cb[jj] - (cb[j] * u[jj - j - 1]) * p
            if k < 15:
                m = c[j] * p
                for jj in range(j + 1, 8):
                    c[jj] = c[jj] - m * u[jj - j - 1]
                for jj in range(8):
                    nb[jj] = nb[jj] - m * row_of(c[j], jj)
            if j < 7:
                m = jnp.where(sub > j, cb[j] * p, 0.0)
                rows = rows - m * row_of(rows, j)
                for jj in range(j + 1):
                    wc[jj] = wc[jj] - m * row_of(wc[jj], j)
        w[lo:lo + 8, :] = jnp.where(lane <= lo + sub, rows, 0.0) * lax.rsqrt(diag)
        if k < 15:
            scaled = [row_of(rows, j) * piv[j] for j in range(8)]
            ys = []
            for j in range(8):
                y = scaled[j]
                for jj in range(j + 1, 8):
                    y = y + row_of(wc[j], jj) * scaled[jj]
                ys.append(y)
            for t in range(k + 1, 16):
                old = at[8 * t:8 * t + 8, :]
                cols = first if t == k + 1 else columns(old, lo)
                parts = [cols[j] * ys[j] for j in range(8)]
                while len(parts) > 1:
                    parts = [a + b for a, b in zip(parts[::2], parts[1::2])]
                at[8 * t:8 * t + 8, :] = jnp.where(inblk, 0.0, old) - parts[0]
            cb = nb
        if hook is not None and k % 4 == 3:
            hook(k // 4)


def hdot(a, b, ca=1, cb=0):
    return lax.dot_general(a, b, (((ca,), (cb,)), ((), ())), precision=HI, preferred_element_type=F32)

def bdot(a, b, ca=1, cb=0):
    return lax.dot_general(a, b, (((ca,), (cb,)), ((), ())), preferred_element_type=F32)

def load_chunk(s, g, lf, lr):
    cut = slice(128 * s, 128 * (s + 1))
    for c in range(8):
        lr[cut, 128 * c:128 * (c + 1)] = g[c // 2, c % 2, s, 128:256, :]
        f = jnp.maximum(g[c // 2, c % 2, s, 0:128, :], 0)
        lf[cut, 128 * c:128 * (c + 1)] = f.T


def gram(lf, lr, rows, cols):
    return bdot(lf[rows, :], lf[cols, :], 1, 1) * (1.0 / 1024) - bdot(lr[rows, :], lr[cols, :], 1, 1)


def ridged(x, first_row, first_col, ridge):
    row = lax.broadcasted_iota(jnp.int32, x.shape, 0) + first_row
    col = lax.broadcasted_iota(jnp.int32, x.shape, 1) + first_col
    return x + jnp.where(row == col, ridge, 0.0)


def half_block(g, core):
    total = jnp.zeros((128, 128), F32)
    rest = jnp.zeros((128, 128), F32)
    for z in range(4):
        f = jnp.maximum(g[z, core, 0, 0:128, :], 0)
        r = g[z, core, 0, 128:256, :]
        total = total + bdot(f, f, 0, 0)
        rest = rest + bdot(r, r, 1, 1)
    return total * (1.0 / 1024) - rest


def second_block(w, lf, lr, u01, at, ridge):
    d = gram(lf, lr, slice(0, 256), slice(128, 256))
    x = hdot(w[...], d[:128, :])
    u01[...] = x
    at[...] = ridged(d[128:, :], 0, 0, ridge) - hdot(x, x, 0, 0)


def first_panels(cols, w0, w, u01, aug):
    x0 = hdot(w0[...], aug[0:128, cols])
    x1 = hdot(w[...], aug[128:256, cols] - hdot(u01[...], x0, 0, 0))
    aug[0:128, cols] = x0
    aug[128:256, cols] = x1
    return x0, x1


def strip(w0, w, u01, lf, lr, xf, xr, aug, fin, ridge, first_col):
    cols = slice(256, 512)
    part = bdot(lf[...], jnp.maximum(xf[...], 0)) * (1.0 / 1024) - bdot(lr[...], xr[...], 1, 1)
    aug[:, cols] = ridged(part, 0, first_col, ridge)
    x0, x1 = first_panels(cols, w0, w, u01, aug)
    fin[0] = x0
    fin[1] = x1


def third_block(w0, w, u01, lf, lr, aug, at, ridge):
    cols = slice(0, 256)
    aug[:, cols] = ridged(gram(lf, lr, slice(0, 512), slice(256, 512)), 0, 256, ridge)
    first_panels(cols, w0, w, u01, aug)
    left = aug[0:256, 0:128]
    at[...] = aug[256:384, 0:128] - hdot(left, left, 0, 0)


def lower_panels(aug):
    aug[256:384, 128:512] = aug[256:384, 128:512] - hdot(aug[0:256, 0:128], aug[0:256, 128:512], 0, 0)
    aug[384:512, 128:512] = aug[384:512, 128:512] - hdot(aug[0:256, 128:256], aug[0:256, 128:512], 0, 0)


def last_panel(w, aug, at, left, fin):
    x = hdot(w[...], aug[256:384, 128:512])
    fin[2] = x[:, 128:384]
    u = x[:, 0:128]
    at[...] = aug[384:512, 128:256] - hdot(u, u, 0, 0)
    left[...] = aug[384:512, 256:512] - hdot(u, x[:, 128:384], 0, 0)


MESH = pl.DeviceIdType.MESH


def remote(src, dst, send, recv, row, col):
    return pltpu.make_async_remote_copy(
        src_ref=src, dst_ref=dst, send_sem=send, recv_sem=recv, device_id=(row, col), device_id_type=MESH
    )


def kernel(pre, res, rd, out, g, xf, xr, lf, lr, aug, u01, half, left, at, w0, w1, w, fin, loc, sent, r1, r2, r3, r4, r5, r6, s7):
    row = lax.axis_index("row")
    col = lax.axis_index("col")
    zhi = lax.rem(row, 2)
    spot = row // 2
    zlo = col // 2
    core = lax.rem(col, 2)
    deep = zhi * 4 + zlo
    other = col + 1 - 2 * core
    ridge = rd[0]
    first_col = row * 2048 + col * 256
    sub = lax.broadcasted_iota(jnp.int32, (8, 128), 0)
    lane = lax.broadcasted_iota(jnp.int32, (8, 128), 1)

    def in_plane(d):
        return 2 * lax.rem(spot + d, 16) + zhi, col

    def in_ring(d):
        z = lax.rem(deep + d, 8)
        return 2 * spot + z // 4, 2 * lax.rem(z, 4) + core

    barrier = pltpu.get_barrier_semaphore()
    peers = [in_plane(d) for d in range(1, 16)] + [in_ring(d) for d in range(1, 8)]
    peers += [(row, 2 * z + 1 - core) for z in range(4)]
    for peer in peers:
        pl.semaphore_signal(barrier, inc=1, device_id=peer, device_id_type=MESH)
    with jax.named_scope("a_barrier"):
        pl.semaphore_wait(barrier, len(peers))

    def piece(q, p):
        if p < 8:
            return pre.at[16 * p:16 * p + 16, 128 * q:128 * q + 128]
        return res.at[128 * q + 16 * (p - 8):128 * q + 16 * (p - 8) + 16, :]

    def scatter(q, p):
        return remote(piece(q, p), g.at[zlo, core, q, 16 * p:16 * p + 16, :], sent.at[0], r1.at[q], 2 * p, col)

    def own(q):
        return pltpu.make_async_copy(piece(q, 0), g.at[zlo, core, q, 0:16, :], r1.at[q])

    mine = pl.ds(pl.multiple_of(16 * spot, 16), 16)

    def along_ring(q, d):
        ref = g.at[zlo, core, q, mine, :]
        return remote(ref, ref, sent.at[1], r2.at[q], *in_ring(d))

    def across(q, d):
        ref = g.at[:, core, q, mine, :]
        return remote(ref, ref, sent.at[2], r3.at[q], *in_plane(d))

    def to_partner(q):
        ref = g.at[:, core, q]
        return remote(ref, ref, sent.at[3], r4.at[q], row, other)

    def bulk(ref, sem):
        return remote(ref, ref, sem, sem, row, other)

    root = (spot == 0) & (zhi == 0)

    def block_of(to):
        return pl.ds(pl.multiple_of(256 * to, 256), 256)

    home = pl.ds(pl.multiple_of(128 * col, 128), 128)

    def move_cols(d):
        to = lax.rem(col + d, 8)
        return remote(pre.at[:, block_of(to)], xf.at[home, :], sent.at[4], r5.at[0], row, to)

    def move_rows(d):
        to = lax.rem(col + d, 8)
        return remote(res.at[block_of(to), :], xr.at[:, home], sent.at[5], r5.at[1], row, to)

    keep_cols = pltpu.make_async_copy(pre.at[:, block_of(col)], xf.at[home, :], loc.at[0])
    keep_rows = pltpu.make_async_copy(res.at[block_of(col), :], xr.at[:, home], loc.at[1])

    here = pl.ds(pl.multiple_of(256 * col, 256), 256)

    def deliver(q, i):
        to = 4 * lax.rem(q, 2) + i
        return remote(fin.at[q, 32 * i:32 * i + 32, :], out.at[q // 2, :, here], sent.at[6], r6.at[0], row, to)

    def keep(q, i):
        return pltpu.make_async_copy(fin.at[q, 32 * i:32 * i + 32, :], out.at[q // 2, :, here], loc.at[2])

    def send_piece(q, i):
        to = 4 * lax.rem(q, 2) + i

        @pl.when(col == to)
        def _():
            keep(q, i).start()

        @pl.when(col != to)
        def _():
            deliver(q, i).start()

    @pl.when(root)
    def _():
        for q in range(4):
            own(q).start()
            for p in range(1, 16):
                scatter(q, p).start()

    keep_cols.start()
    keep_rows.start()

    def move(kind, offsets):
        for d in offsets:
            kind(d).start()

    move(move_cols, (1, 7))

    def forward_ring(q):
        @pl.when(zhi == 0)
        def _():
            @pl.when(spot == 0)
            def _():
                own(q).wait()

            @pl.when(spot != 0)
            def _():
                scatter(q, 1).wait_recv()

            for d in range(1, 8):
                along_ring(q, d).start()

    def forward_plane(q):
        @pl.when(zhi == 0)
        def _():
            bulk(g.at[0:3, core, q, mine, :], r2.at[q]).wait_recv()

        @pl.when(zhi != 0)
        def _():
            bulk(g.at[:, core, q, mine, :], r2.at[q]).wait_recv()

        for d in range(1, 16):
            across(q, d).start()

    def swap():
        return remote(half.at[0], half.at[1], s7.at[0], s7.at[1], row, other)

    def gathered(q):
        bulk(g.at[:, core, q, 0:240, :], r3.at[q]).wait_recv()

    def share(q):
        gathered(q)
        to_partner(q).start()

    with jax.named_scope("b_ring0"):
        forward_ring(0)
    move(move_cols, (2, 6))
    with jax.named_scope("c_plane0"):
        forward_plane(0)
    with jax.named_scope("d_ring123"):
        for q in range(1, 4):
            forward_ring(q)
    move(move_cols, (3, 4, 5))
    move(move_rows, range(1, 8))
    with jax.named_scope("e_plane1"):
        forward_plane(1)
    with jax.named_scope("f_gathered0"):
        gathered(0)

    def arrived():
        keep_cols.wait()
        keep_rows.wait()
        bulk(xf.at[0:896, :], r5.at[0]).wait_recv()
        bulk(xr.at[:, 0:896], r5.at[1]).wait_recv()

    def hook(q, i):
        if i == 1:
            @pl.when(q < 2)
            def _():
                with jax.named_scope("j_share"):
                    share(q + 1)
        if i == 2:
            @pl.when(q == 1)
            def _():
                with jax.named_scope("j_share"):
                    share(3)
        if i == 0:
            @pl.when(q == 2)
            def _():
                with jax.named_scope("s_arrived"):
                    arrived()
                with jax.named_scope("s_strip"):
                    strip(w0, w1, u01, lf, lr, xf, xr, aug, fin, ridge, first_col)
                for e in range(2):
                    for n in range(4):
                        send_piece(e, n)
                with jax.named_scope("s_lower"):
                    lower_panels(aug)

        @pl.when(q == 3)
        def _():
            fin[3, 32 * i:32 * i + 32, :] = hdot(w[32 * i:32 * i + 32, :], left[...])
            send_piece(3, i)

    def turn(q, carry):
        with jax.named_scope("i_base"):
            base(at, w, sub, lane, lambda i: hook(q, i))

        @pl.when(q == 0)
        def _():
            w0[...] = w[...]
            with jax.named_scope("k_chunk01"):
                for s in range(2):
                    to_partner(s).wait_recv()
                    load_chunk(s, g, lf, lr)
            with jax.named_scope("k_second"):
                second_block(w, lf, lr, u01, at, ridge)

        @pl.when(q == 1)
        def _():
            w1[...] = w[...]
            with jax.named_scope("l_chunk23"):
                for s in range(2, 4):
                    to_partner(s).wait_recv()
                    load_chunk(s, g, lf, lr)
            with jax.named_scope("l_third"):
                third_block(w0, w1, u01, lf, lr, aug, at, ridge)

        @pl.when(q == 2)
        def _():
            with jax.named_scope("m_last"):
                last_panel(w, aug, at, left, fin)
            for i in range(4):
                send_piece(2, i)

        return carry

    with jax.named_scope("g_half"):
        half[0] = half_block(g, core)
    swap().start()
    to_partner(0).start()
    with jax.named_scope("g_plane23"):
        forward_plane(2)
        forward_plane(3)
    with jax.named_scope("h_swap"):
        swap().wait_recv()
    at[...] = ridged(half[0] + half[1], 0, 0, ridge)
    lax.fori_loop(0, 4, turn, 0)

    with jax.named_scope("n_final"):
        bulk(fin.at[:, 0:112, :], r6.at[0]).wait_recv()
    with jax.named_scope("o_sends"):
        pltpu.make_async_copy(fin.at[0, 0:64, :], fin.at[1, 0:64, :], loc.at[2]).wait()
        bulk(fin.at[:, 0:112, :], sent.at[6]).wait_send()
        bulk(xf.at[0:896, :], sent.at[4]).wait_send()
        bulk(xr.at[:, 0:896], sent.at[5]).wait_send()
        swap().wait_send()
        bulk(g.at[:, core], sent.at[3]).wait_send()
        bulk(g.at[:, core, :, 0:240, :], sent.at[2]).wait_send()

        @pl.when(zhi == 0)
        def _():
            bulk(g.at[0, core, :, 0:112, :], sent.at[1]).wait_send()

        @pl.when(root)
        def _():
            bulk(g.at[:, core, 0, 0:240, :], sent.at[0]).wait_send()


def local(preacts, resident, ridge):
    dma = pltpu.SemaphoreType.DMA
    raw = pl.pallas_call(
        kernel,
        out_shape=pltpu.VMEM((2, 32, 2048), F32),
        in_specs=[
            pl.BlockSpec(memory_space=pl.ANY),
            pl.BlockSpec(memory_space=pl.ANY),
            pl.BlockSpec(memory_space=pltpu.SMEM),
        ],
        out_specs=pl.BlockSpec(memory_space=pltpu.VMEM),
        scratch_shapes=[
            pltpu.VMEM((4, 2, 4, 256, 128), B16),
            pltpu.VMEM((1024, 256), B16),
            pltpu.VMEM((256, 1024), B16),
            pltpu.VMEM((512, 1024), B16),
            pltpu.VMEM((512, 1024), B16),
            pltpu.VMEM((512, 512), F32),
            pltpu.VMEM((128, 128), F32),
            pltpu.VMEM((2, 128, 128), F32),
            pltpu.VMEM((128, 256), F32),
            pltpu.VMEM((128, 128), F32),
            pltpu.VMEM((128, 128), F32),
            pltpu.VMEM((128, 128), F32),
            pltpu.VMEM((128, 128), F32),
            pltpu.VMEM((4, 128, 256), F32),
            dma((3,)), dma((7,)),
            dma((4,)), dma((4,)), dma((4,)), dma((4,)),
            dma((2,)), dma((1,)), dma((2,)),
        ],
        compiler_params=pltpu.CompilerParams(collective_id=0, has_side_effects=True),
    )(preacts, resident, ridge)
    column = lax.axis_index("row") * 2048 + lax.broadcasted_iota(jnp.int32, raw.shape, 2)
    line = lax.broadcasted_iota(jnp.int32, raw.shape, 0) * 256 + lax.broadcasted_iota(jnp.int32, raw.shape, 1)
    return jnp.where(column >= line + lax.axis_index("col") * 32, raw, 0.0)


def solution(mesh):
    placed = (P("col", "row"), P("row", "col"), P())
    return jax.shard_map(
        local, mesh=mesh, in_specs=placed, out_specs=P(None, "col", "row"), check_vma=False
    )
```

```python
import jax
import jax.numpy as jnp
from jax import lax
from jax.experimental import pallas as pl
from jax.experimental.pallas import tpu as pltpu
from jax.sharding import PartitionSpec as P

HI = lax.Precision.HIGHEST
F32 = jnp.float32
B16 = jnp.bfloat16

def full(x):
    return jnp.broadcast_to(x, (8, 128))

def row_of(x, j):
    return full(x[j:j + 1, :])


def columns(tile, lo):
    return [full(tile[:, lo + j:lo + j + 1]) for j in range(8)]


def base(at, w, sub, lane, hook):
    cb = columns(at[0:8, :], 0)
    for k in range(16):
        lo = 8 * k
        tile = at[lo:lo + 8, :]
        inblk = (lane >= lo) & (lane < lo + 8)
        rows = jnp.where(inblk, jnp.where(lane - lo == sub, 1.0, 0.0), tile)
        wc = [jnp.where(sub == j, 1.0, 0.0).astype(F32) for j in range(8)]
        if k < 15:
            below = at[lo + 8:lo + 16, :]
            first = columns(below, lo)
            nb = columns(below, lo + 8)
            c = list(first)
        piv = []
        diag = jnp.zeros((8, 128), F32)
        for j in range(8):
            d = row_of(cb[j], j)
            p = 1.0 / d
            piv.append(p)
            diag = jnp.where(sub == j, d, diag)
            u = [row_of(cb[j], jj) for jj in range(j + 1, 8)]
            for jj in range(j + 1, 8):
                cb[jj] = cb[jj] - (cb[j] * u[jj - j - 1]) * p
            if k < 15:
                m = c[j] * p
                for jj in range(j + 1, 8):
                    c[jj] = c[jj] - m * u[jj - j - 1]
                for jj in range(8):
                    nb[jj] = nb[jj] - m * row_of(c[j], jj)
            if j < 7:
                m = jnp.where(sub > j, cb[j] * p, 0.0)
                rows = rows - m * row_of(rows, j)
                for jj in range(j + 1):
                    wc[jj] = wc[jj] - m * row_of(wc[jj], j)
        w[lo:lo + 8, :] = jnp.where(lane <= lo + sub, rows, 0.0) * lax.rsqrt(diag)
        if k < 15:
            scaled = [row_of(rows, j) * piv[j] for j in range(8)]
            ys = []
            for j in range(8):
                y = scaled[j]
                for jj in range(j + 1, 8):
                    y = y + row_of(wc[j], jj) * scaled[jj]
                ys.append(y)
            for t in range(k + 1, 16):
                old = at[8 * t:8 * t + 8, :]
                cols = first if t == k + 1 else columns(old, lo)
                parts = [cols[j] * ys[j] for j in range(8)]
                while len(parts) > 1:
                    parts = [a + b for a, b in zip(parts[::2], parts[1::2])]
                at[8 * t:8 * t + 8, :] = jnp.where(inblk, 0.0, old) - parts[0]
            cb = nb
        if k % 4 == 3:
            hook(k // 4)


def hdot(a, b, ca=1, cb=0):
    if b.shape[1 - cb] < 256:
        return lax.dot_general(a, b, (((ca,), (cb,)), ((), ())), precision=HI, preferred_element_type=F32)
    a0, a1, a2 = thirds(a)
    b0, b1, b2 = thirds(b)
    left = jnp.concatenate([a0, a0, a0, a1, a1, a2], axis=ca)
    right = jnp.concatenate([b0, b1, b2, b0, b1, b0], axis=cb)
    return bdot(left, right, ca, cb)


def thirds(x):
    x0 = x.astype(B16)
    rest = x - x0.astype(F32)
    x1 = rest.astype(B16)
    return x0, x1, (rest - x1.astype(F32)).astype(B16)


def bdot(a, b, ca=1, cb=0):
    return lax.dot_general(a, b, (((ca,), (cb,)), ((), ())), preferred_element_type=F32)

def load_chunk(s, g, lf, lr):
    cut = slice(128 * s, 128 * (s + 1))
    for c in range(8):
        lr[cut, 128 * c:128 * (c + 1)] = g[c // 2, c % 2, s, 128:256, :]
        f = jnp.maximum(g[c // 2, c % 2, s, 0:128, :], 0)
        lf[cut, 128 * c:128 * (c + 1)] = f.T


def gram(lf, lr, rows, cols):
    return bdot(lf[rows, :], lf[cols, :], 1, 1) * (1.0 / 1024) - bdot(lr[rows, :], lr[cols, :], 1, 1)


def ridged(x, first_row, first_col, ridge):
    row = lax.broadcasted_iota(jnp.int32, x.shape, 0) + first_row
    col = lax.broadcasted_iota(jnp.int32, x.shape, 1) + first_col
    return x + jnp.where(row == col, ridge, 0.0)


def half_block(g, core):
    total = jnp.zeros((128, 128), F32)
    rest = jnp.zeros((128, 128), F32)
    for z in range(4):
        f = jnp.maximum(g[z, core, 0, 0:128, :], 0)
        r = g[z, core, 0, 128:256, :]
        total = total + bdot(f, f, 0, 0)
        rest = rest + bdot(r, r, 1, 1)
    return total * (1.0 / 1024) - rest


def second_block(w, lf, lr, u01, at, ridge):
    d = gram(lf, lr, slice(0, 256), slice(128, 256))
    x = hdot(w[...], d[:128, :])
    u01[...] = x
    at[...] = ridged(d[128:, :], 0, 0, ridge) - hdot(x, x, 0, 0)


def first_panels(cols, w0, w, u01, aug):
    x0 = hdot(w0[...], aug[0:128, cols])
    x1 = hdot(w[...], aug[128:256, cols] - hdot(u01[...], x0, 0, 0))
    aug[0:128, cols] = x0
    aug[128:256, cols] = x1
    return x0, x1


def strip(rows, lf, lr, xf, xr, aug, ridge, first_col):
    part = bdot(lf[rows, :], jnp.maximum(xf[...], 0)) * (1.0 / 1024) - bdot(lr[rows, :], xr[...], 1, 1)
    aug[rows, 256:512] = ridged(part, rows.start, first_col, ridge)


def upper_strip(w0, w, u01, lf, lr, xf, xr, aug, fin, ridge, first_col):
    strip(slice(0, 256), lf, lr, xf, xr, aug, ridge, first_col)
    x0, x1 = first_panels(slice(256, 512), w0, w, u01, aug)
    fin[0] = x0
    fin[1] = x1


def third_block(w0, w, u01, lf, lr, aug, at, ridge):
    cols = slice(0, 128)
    aug[0:384, cols] = ridged(gram(lf, lr, slice(0, 384), slice(256, 384)), 0, 256, ridge)
    first_panels(cols, w0, w, u01, aug)
    left = aug[0:256, cols]
    at[...] = aug[256:384, cols] - hdot(left, left, 0, 0)


def lower_panels(w0, w, u01, lf, lr, xf, xr, aug, ridge, first_col):
    cols = slice(128, 256)
    aug[:, cols] = ridged(gram(lf, lr, slice(0, 512), slice(384, 512)), 0, 384, ridge)
    first_panels(cols, w0, w, u01, aug)
    strip(slice(256, 512), lf, lr, xf, xr, aug, ridge, first_col)
    aug[256:384, 128:512] = aug[256:384, 128:512] - hdot(aug[0:256, 0:128], aug[0:256, 128:512], 0, 0)
    aug[384:512, 128:512] = aug[384:512, 128:512] - hdot(aug[0:256, 128:256], aug[0:256, 128:512], 0, 0)


def last_panel(w, aug, at, left, fin):
    x = hdot(w[...], aug[256:384, 128:512])
    fin[2] = x[:, 128:384]
    u = x[:, 0:128]
    at[...] = aug[384:512, 128:256] - hdot(u, u, 0, 0)
    left[...] = aug[384:512, 256:512] - hdot(u, x[:, 128:384], 0, 0)


MESH = pl.DeviceIdType.MESH


def remote(src, dst, send, recv, row, col):
    return pltpu.make_async_remote_copy(
        src_ref=src, dst_ref=dst, send_sem=send, recv_sem=recv, device_id=(row, col), device_id_type=MESH
    )


def kernel(pre, res, rd, out, g, xf, xr, lf, lr, aug, u01, half, left, at, w0, w1, w, fin, loc, sent, r1, r2, r3, r4, r5, r6, s7):
    row = lax.axis_index("row")
    col = lax.axis_index("col")
    zhi = lax.rem(row, 2)
    spot = row // 2
    zlo = col // 2
    core = lax.rem(col, 2)
    deep = zhi * 4 + zlo
    other = col + 1 - 2 * core
    ridge = rd[0]
    first_col = row * 2048 + col * 256
    sub = lax.broadcasted_iota(jnp.int32, (8, 128), 0)
    lane = lax.broadcasted_iota(jnp.int32, (8, 128), 1)

    def in_plane(d):
        return 2 * lax.rem(spot + d, 16) + zhi, col

    def in_ring(d):
        z = lax.rem(deep + d, 8)
        return 2 * spot + z // 4, 2 * lax.rem(z, 4) + core

    barrier = pltpu.get_barrier_semaphore()
    peers = [in_plane(d) for d in range(1, 16)] + [in_ring(d) for d in range(1, 8)]
    peers += [(row, 2 * z + 1 - core) for z in range(4)]
    for peer in peers:
        pl.semaphore_signal(barrier, inc=1, device_id=peer, device_id_type=MESH)
    with jax.named_scope("a_barrier"):
        pl.semaphore_wait(barrier, len(peers))

    def piece(q, p):
        if p < 8:
            return pre.at[16 * p:16 * p + 16, 128 * q:128 * q + 128]
        return res.at[128 * q + 16 * (p - 8):128 * q + 16 * (p - 8) + 16, :]

    def scatter(q, p):
        return remote(piece(q, p), g.at[zlo, core, q, 16 * p:16 * p + 16, :], sent.at[0], r1.at[q], 2 * p, col)

    def own(q):
        return pltpu.make_async_copy(piece(q, 0), g.at[zlo, core, q, 0:16, :], r1.at[q])

    mine = pl.ds(pl.multiple_of(16 * spot, 16), 16)

    def along_ring(q, d):
        ref = g.at[zlo, core, q, mine, :]
        return remote(ref, ref, sent.at[1], r2.at[q], *in_ring(d))

    def across(q, d):
        ref = g.at[:, core, q, mine, :]
        return remote(ref, ref, sent.at[2], r3.at[q], *in_plane(d))

    def to_partner(q):
        ref = g.at[:, core, q]
        return remote(ref, ref, sent.at[3], r4.at[q], row, other)

    def bulk(ref, sem):
        return remote(ref, ref, sem, sem, row, other)

    root = (spot == 0) & (zhi == 0)

    def block_of(to):
        return pl.ds(pl.multiple_of(256 * to, 256), 256)

    home = pl.ds(pl.multiple_of(128 * col, 128), 128)

    def move_cols(d):
        to = lax.rem(col + d, 8)
        return remote(pre.at[:, block_of(to)], xf.at[home, :], sent.at[4], r5.at[0], row, to)

    def move_rows(d):
        to = lax.rem(col + d, 8)
        return remote(res.at[block_of(to), :], xr.at[:, home], sent.at[5], r5.at[1], row, to)

    keep_cols = pltpu.make_async_copy(pre.at[:, block_of(col)], xf.at[home, :], loc.at[0])
    keep_rows = pltpu.make_async_copy(res.at[block_of(col), :], xr.at[:, home], loc.at[1])

    here = pl.ds(pl.multiple_of(256 * col, 256), 256)

    def deliver(q, i):
        to = 4 * (q % 2) + i
        return remote(fin.at[q, 32 * i:32 * i + 32, :], out.at[q // 2, :, here], sent.at[6], r6.at[0], row, to)

    def keep(q, i):
        return pltpu.make_async_copy(fin.at[q, 32 * i:32 * i + 32, :], out.at[q // 2, :, here], loc.at[2])

    def send_piece(q, i):
        to = 4 * (q % 2) + i

        @pl.when(col == to)
        def _():
            keep(q, i).start()

        @pl.when(col != to)
        def _():
            deliver(q, i).start()

    @pl.when(root)
    def _():
        for q in range(4):
            own(q).start()
            for p in range(1, 16):
                scatter(q, p).start()

    keep_cols.start()
    keep_rows.start()

    def move(kind, offsets):
        for d in offsets:
            kind(d).start()

    @pl.when(zhi != 0)
    def _():
        move(move_cols, range(1, 8))
        move(move_rows, range(1, 8))

    @pl.when(zhi == 0)
    def _():
        move(move_cols, (1, 7))

    def forward_ring(q):
        @pl.when(zhi == 0)
        def _():
            @pl.when(spot == 0)
            def _():
                own(q).wait()

            @pl.when(spot != 0)
            def _():
                scatter(q, 1).wait_recv()

            for d in range(1, 8):
                along_ring(q, d).start()

    def forward_plane(q):
        @pl.when(zhi == 0)
        def _():
            bulk(g.at[0:3, core, q, mine, :], r2.at[q]).wait_recv()

        @pl.when(zhi != 0)
        def _():
            bulk(g.at[:, core, q, mine, :], r2.at[q]).wait_recv()

        for d in range(1, 16):
            across(q, d).start()

    def swap():
        return remote(half.at[0], half.at[1], s7.at[0], s7.at[1], row, other)

    def gathered(q):
        bulk(g.at[:, core, q, 0:240, :], r3.at[q]).wait_recv()

    def share(q):
        gathered(q)
        to_partner(q).start()

    with jax.named_scope("b_ring0"):
        forward_ring(0)

    @pl.when(zhi == 0)
    def _():
        move(move_cols, (2, 6, 4))

    with jax.named_scope("c_plane0"):
        forward_plane(0)
    with jax.named_scope("d_ring123"):
        for q in range(1, 4):
            forward_ring(q)

    @pl.when(zhi == 0)
    def _():
        move(move_cols, (3, 5))
        move(move_rows, range(1, 8))

    with jax.named_scope("e_plane1"):
        forward_plane(1)
    with jax.named_scope("f_gathered0"):
        gathered(0)

    def arrived():
        keep_cols.wait()
        keep_rows.wait()
        bulk(xf.at[0:896, :], r5.at[0]).wait_recv()
        bulk(xr.at[:, 0:896], r5.at[1]).wait_recv()

    def early_hook(q, i):
        if i == 1:
            with jax.named_scope("j_share"):
                share(q + 1)
        if i == 2:
            @pl.when(q == 1)
            def _():
                with jax.named_scope("j_share3"):
                    share(3)

    def turn(q, carry):
        with jax.named_scope("i_base"):
            base(at, w, sub, lane, lambda i: early_hook(q, i))

        @pl.when(q == 0)
        def _():
            w0[...] = w[...]
            with jax.named_scope("k_chunk01"):
                for s in range(2):
                    to_partner(s).wait_recv()
                    load_chunk(s, g, lf, lr)
            with jax.named_scope("k_second"):
                second_block(w, lf, lr, u01, at, ridge)

        return carry

    def third_hook(i):
        if i == 1:
            for e in range(2):
                for n in range(4):
                    send_piece(e, n)
            to_partner(3).wait_recv()
            load_chunk(3, g, lf, lr)
            lower_panels(w0, w1, u01, lf, lr, xf, xr, aug, ridge, first_col)

    def finish(n):
        rows = slice(32 * n, 32 * n + 32)
        fin[3, rows, :] = hdot(w[rows, :], left[...])

    def last_hook(i):
        if i > 0:
            send_piece(3, i - 1)
        finish(i)
        if i == 3:
            send_piece(3, 3)

    with jax.named_scope("g_half"):
        half[0] = half_block(g, core)
    swap().start()
    to_partner(0).start()
    with jax.named_scope("g_plane23"):
        forward_plane(2)
        forward_plane(3)
    with jax.named_scope("h_swap"):
        swap().wait_recv()
    at[...] = ridged(half[0] + half[1], 0, 0, ridge)
    lax.fori_loop(0, 2, turn, 0)
    w1[...] = w[...]
    with jax.named_scope("l_chunk2"):
        to_partner(2).wait_recv()
        load_chunk(2, g, lf, lr)
    with jax.named_scope("l_third"):
        third_block(w0, w1, u01, lf, lr, aug, at, ridge)
    with jax.named_scope("l_arrived"):
        arrived()
    with jax.named_scope("l_base2"):
        upper_strip(w0, w1, u01, lf, lr, xf, xr, aug, fin, ridge, first_col)
        base(at, w, sub, lane, third_hook)
    with jax.named_scope("m_last"):
        last_panel(w, aug, at, left, fin)
    for n in range(4):
        send_piece(2, n)
    with jax.named_scope("m_base3"):
        base(at, w, sub, lane, last_hook)

    with jax.named_scope("n_final"):
        bulk(fin.at[:, 0:112, :], r6.at[0]).wait_recv()
    with jax.named_scope("o_sends"):
        pltpu.make_async_copy(fin.at[0, 0:64, :], fin.at[1, 0:64, :], loc.at[2]).wait()
        bulk(fin.at[:, 0:112, :], sent.at[6]).wait_send()
        bulk(xf.at[0:896, :], sent.at[4]).wait_send()
        bulk(xr.at[:, 0:896], sent.at[5]).wait_send()
        swap().wait_send()
        bulk(g.at[:, core], sent.at[3]).wait_send()
        bulk(g.at[:, core, :, 0:240, :], sent.at[2]).wait_send()

        @pl.when(zhi == 0)
        def _():
            bulk(g.at[0, core, :, 0:112, :], sent.at[1]).wait_send()

        @pl.when(root)
        def _():
            bulk(g.at[:, core, 0, 0:240, :], sent.at[0]).wait_send()


def local(preacts, resident, ridge):
    dma = pltpu.SemaphoreType.DMA
    raw = pl.pallas_call(
        kernel,
        out_shape=pltpu.VMEM((2, 32, 2048), F32),
        in_specs=[
            pl.BlockSpec(memory_space=pl.ANY),
            pl.BlockSpec(memory_space=pl.ANY),
            pl.BlockSpec(memory_space=pltpu.SMEM),
        ],
        out_specs=pl.BlockSpec(memory_space=pltpu.VMEM),
        scratch_shapes=[
            pltpu.VMEM((4, 2, 4, 256, 128), B16),
            pltpu.VMEM((1024, 256), B16),
            pltpu.VMEM((256, 1024), B16),
            pltpu.VMEM((512, 1024), B16),
            pltpu.VMEM((512, 1024), B16),
            pltpu.VMEM((512, 512), F32),
            pltpu.VMEM((128, 128), F32),
            pltpu.VMEM((2, 128, 128), F32),
            pltpu.VMEM((128, 256), F32),
            pltpu.VMEM((128, 128), F32),
            pltpu.VMEM((128, 128), F32),
            pltpu.VMEM((128, 128), F32),
            pltpu.VMEM((128, 128), F32),
            pltpu.VMEM((4, 128, 256), F32),
            dma((3,)), dma((7,)),
            dma((4,)), dma((4,)), dma((4,)), dma((4,)),
            dma((2,)), dma((1,)), dma((2,)),
        ],
        compiler_params=pltpu.CompilerParams(collective_id=0, has_side_effects=True),
    )(preacts, resident, ridge)
    column = lax.axis_index("row") * 2048 + lax.broadcasted_iota(jnp.int32, raw.shape, 2)
    line = lax.broadcasted_iota(jnp.int32, raw.shape, 0) * 256 + lax.broadcasted_iota(jnp.int32, raw.shape, 1)
    return jnp.where(column >= line + lax.axis_index("col") * 32, raw, 0.0)


def solution(mesh):
    placed = (P("col", "row"), P("row", "col"), P())
    return jax.shard_map(
        local, mesh=mesh, in_specs=placed, out_specs=P(None, "col", "row"), check_vma=False
    )
```

```python
import jax
import jax.numpy as jnp
from jax import lax
from jax.experimental import pallas as pl
from jax.experimental.pallas import tpu as pltpu
from jax.sharding import PartitionSpec as P

HI = lax.Precision.HIGHEST
F32 = jnp.float32
B16 = jnp.bfloat16

def full(x):
    return jnp.broadcast_to(x, (8, 128))

def row_of(x, j):
    return full(x[j:j + 1, :])


def columns(tile, lo):
    return [full(tile[:, lo + j:lo + j + 1]) for j in range(8)]


def base(at, w, sub, lane, hook):
    cb = columns(at[0:8, :], 0)
    for k in range(16):
        lo = 8 * k
        tile = at[lo:lo + 8, :]
        inblk = (lane >= lo) & (lane < lo + 8)
        rows = jnp.where(inblk, jnp.where(lane - lo == sub, 1.0, 0.0), tile)
        wc = [jnp.where(sub == j, 1.0, 0.0).astype(F32) for j in range(8)]
        if k < 15:
            below = at[lo + 8:lo + 16, :]
            first = columns(below, lo)
            nb = columns(below, lo + 8)
            c = list(first)
        piv = []
        diag = jnp.zeros((8, 128), F32)
        for j in range(8):
            d = row_of(cb[j], j)
            p = 1.0 / d
            piv.append(p)
            diag = jnp.where(sub == j, d, diag)
            u = [row_of(cb[j], jj) for jj in range(j + 1, 8)]
            for jj in range(j + 1, 8):
                cb[jj] = cb[jj] - (cb[j] * u[jj - j - 1]) * p
            if k < 15:
                m = c[j] * p
                for jj in range(j + 1, 8):
                    c[jj] = c[jj] - m * u[jj - j - 1]
                for jj in range(8):
                    nb[jj] = nb[jj] - m * row_of(c[j], jj)
            if j < 7:
                m = jnp.where(sub > j, cb[j] * p, 0.0)
                rows = rows - m * row_of(rows, j)
                for jj in range(j + 1):
                    wc[jj] = wc[jj] - m * row_of(wc[jj], j)
        w[lo:lo + 8, :] = jnp.where(lane <= lo + sub, rows, 0.0) * lax.rsqrt(diag)
        if k < 15:
            scaled = [row_of(rows, j) * piv[j] for j in range(8)]
            ys = []
            for j in range(8):
                y = scaled[j]
                for jj in range(j + 1, 8):
                    y = y + row_of(wc[j], jj) * scaled[jj]
                ys.append(y)
            for t in range(k + 1, 16):
                old = at[8 * t:8 * t + 8, :]
                cols = first if t == k + 1 else columns(old, lo)
                parts = [cols[j] * ys[j] for j in range(8)]
                while len(parts) > 1:
                    parts = [a + b for a, b in zip(parts[::2], parts[1::2])]
                at[8 * t:8 * t + 8, :] = jnp.where(inblk, 0.0, old) - parts[0]
            cb = nb
        if k % 4 == 3:
            hook(k // 4)


def hdot(a, b, ca=1, cb=0):
    if b.shape[1 - cb] < 256:
        return lax.dot_general(a, b, (((ca,), (cb,)), ((), ())), precision=HI, preferred_element_type=F32)
    a0, a1, a2 = thirds(a)
    b0, b1, b2 = thirds(b)
    left = jnp.concatenate([a0, a0, a0, a1, a1, a2], axis=ca)
    right = jnp.concatenate([b0, b1, b2, b0, b1, b0], axis=cb)
    return bdot(left, right, ca, cb)


def thirds(x):
    x0 = x.astype(B16)
    rest = x - x0.astype(F32)
    x1 = rest.astype(B16)
    return x0, x1, (rest - x1.astype(F32)).astype(B16)


def bdot(a, b, ca=1, cb=0):
    return lax.dot_general(a, b, (((ca,), (cb,)), ((), ())), preferred_element_type=F32)

def load_chunk(s, g, lf, lr):
    cut = slice(128 * s, 128 * (s + 1))
    for c in range(8):
        lr[cut, 128 * c:128 * (c + 1)] = g[c // 2, c % 2, s, 128:256, :]
        f = jnp.maximum(g[c // 2, c % 2, s, 0:128, :], 0)
        lf[cut, 128 * c:128 * (c + 1)] = f.T


def gram(lf, lr, rows, cols):
    return bdot(lf[rows, :], lf[cols, :], 1, 1) * (1.0 / 1024) - bdot(lr[rows, :], lr[cols, :], 1, 1)


def ridged(x, first_row, first_col, ridge):
    row = lax.broadcasted_iota(jnp.int32, x.shape, 0) + first_row
    col = lax.broadcasted_iota(jnp.int32, x.shape, 1) + first_col
    return x + jnp.where(row == col, ridge, 0.0)


def half_block(g, core):
    total = jnp.zeros((128, 128), F32)
    rest = jnp.zeros((128, 128), F32)
    for z in range(4):
        f = jnp.maximum(g[z, core, 0, 0:128, :], 0)
        r = g[z, core, 0, 128:256, :]
        total = total + bdot(f, f, 0, 0)
        rest = rest + bdot(r, r, 1, 1)
    return total * (1.0 / 1024) - rest


def second_block(w, lf, lr, u01, at, ridge):
    d = gram(lf, lr, slice(0, 256), slice(128, 256))
    x = hdot(w[...], d[:128, :])
    u01[...] = x
    at[...] = ridged(d[128:, :], 0, 0, ridge) - hdot(x, x, 0, 0)


def first_panels(cols, w0, w, u01, aug):
    x0 = hdot(w0[...], aug[0:128, cols])
    x1 = hdot(w[...], aug[128:256, cols] - hdot(u01[...], x0, 0, 0))
    aug[0:128, cols] = x0
    aug[128:256, cols] = x1
    return x0, x1


def strip(rows, lf, lr, xf, xr, aug, ridge, first_col):
    part = bdot(lf[rows, :], jnp.maximum(xf[...], 0)) * (1.0 / 1024) - bdot(lr[rows, :], xr[...], 1, 1)
    aug[rows, 256:512] = ridged(part, rows.start, first_col, ridge)


def upper_strip(w0, w, u01, lf, lr, xf, xr, aug, fin, ridge, first_col):
    strip(slice(0, 256), lf, lr, xf, xr, aug, ridge, first_col)
    x0, x1 = first_panels(slice(256, 512), w0, w, u01, aug)
    fin[0] = x0
    fin[1] = x1


def third_block(w0, w, u01, lf, lr, aug, at, ridge):
    cols = slice(0, 128)
    aug[0:384, cols] = ridged(gram(lf, lr, slice(0, 384), slice(256, 384)), 0, 256, ridge)
    first_panels(cols, w0, w, u01, aug)
    left = aug[0:256, cols]
    at[...] = aug[256:384, cols] - hdot(left, left, 0, 0)


def lower_panels(w0, w, u01, lf, lr, xf, xr, aug, ridge, first_col):
    cols = slice(128, 256)
    aug[:, cols] = ridged(gram(lf, lr, slice(0, 512), slice(384, 512)), 0, 384, ridge)
    first_panels(cols, w0, w, u01, aug)
    strip(slice(256, 512), lf, lr, xf, xr, aug, ridge, first_col)
    aug[256:384, 128:512] = aug[256:384, 128:512] - hdot(aug[0:256, 0:128], aug[0:256, 128:512], 0, 0)
    aug[384:512, 128:512] = aug[384:512, 128:512] - hdot(aug[0:256, 128:256], aug[0:256, 128:512], 0, 0)


def last_panel(w, aug, at, left, fin):
    x = hdot(w[...], aug[256:384, 128:512])
    fin[2] = x[:, 128:384]
    u = x[:, 0:128]
    at[...] = aug[384:512, 128:256] - hdot(u, u, 0, 0)
    left[...] = aug[384:512, 256:512] - hdot(u, x[:, 128:384], 0, 0)


MESH = pl.DeviceIdType.MESH


def remote(src, dst, send, recv, row, col):
    return pltpu.make_async_remote_copy(
        src_ref=src, dst_ref=dst, send_sem=send, recv_sem=recv, device_id=(row, col), device_id_type=MESH
    )


def kernel(pre, res, rd, out, g, xf, xr, lf, lr, aug, u01, half, left, at, w0, w1, w, fin, loc, sent, r1, r2, r3, r4, r5, r6, s7):
    row = lax.axis_index("row")
    col = lax.axis_index("col")
    zhi = lax.rem(row, 2)
    spot = row // 2
    zlo = col // 2
    core = lax.rem(col, 2)
    deep = zhi * 4 + zlo
    other = col + 1 - 2 * core
    ridge = rd[0]
    first_col = row * 2048 + col * 256
    sub = lax.broadcasted_iota(jnp.int32, (8, 128), 0)
    lane = lax.broadcasted_iota(jnp.int32, (8, 128), 1)

    def in_plane(d):
        return 2 * lax.rem(spot + d, 16) + zhi, col

    def in_ring(d):
        z = lax.rem(deep + d, 8)
        return 2 * spot + z // 4, 2 * lax.rem(z, 4) + core

    barrier = pltpu.get_barrier_semaphore()
    peers = [in_plane(d) for d in range(1, 16)] + [in_ring(d) for d in range(1, 8)]
    peers += [(row, 2 * z + 1 - core) for z in range(4)]
    for peer in peers:
        pl.semaphore_signal(barrier, inc=1, device_id=peer, device_id_type=MESH)
    with jax.named_scope("a_barrier"):
        pl.semaphore_wait(barrier, len(peers))

    def piece(q, p):
        if p < 8:
            return pre.at[16 * p:16 * p + 16, 128 * q:128 * q + 128]
        return res.at[128 * q + 16 * (p - 8):128 * q + 16 * (p - 8) + 16, :]

    def scatter(q, p):
        return remote(piece(q, p), g.at[zlo, core, q, 16 * p:16 * p + 16, :], sent.at[0], r1.at[q], 2 * p, col)

    def own(q):
        return pltpu.make_async_copy(piece(q, 0), g.at[zlo, core, q, 0:16, :], r1.at[q])

    mine = pl.ds(pl.multiple_of(16 * spot, 16), 16)

    def along_ring(q, d):
        ref = g.at[zlo, core, q, mine, :]
        return remote(ref, ref, sent.at[1], r2.at[q], *in_ring(d))

    def across(q, d):
        ref = g.at[:, core, q, mine, :]
        return remote(ref, ref, sent.at[2], r3.at[q], *in_plane(d))

    def to_partner(q):
        ref = g.at[:, core, q]
        return remote(ref, ref, sent.at[3], r4.at[q], row, other)

    def bulk(ref, sem):
        return remote(ref, ref, sem, sem, row, other)

    root = (spot == 0) & (zhi == 0)

    def block_of(to):
        return pl.ds(pl.multiple_of(256 * to, 256), 256)

    home = pl.ds(pl.multiple_of(128 * col, 128), 128)

    def move_cols(d):
        to = lax.rem(col + d, 8)
        return remote(pre.at[:, block_of(to)], xf.at[home, :], sent.at[4], r5.at[0], row, to)

    def move_rows(d):
        to = lax.rem(col + d, 8)
        return remote(res.at[block_of(to), :], xr.at[:, home], sent.at[5], r5.at[1], row, to)

    keep_cols = pltpu.make_async_copy(pre.at[:, block_of(col)], xf.at[home, :], loc.at[0])
    keep_rows = pltpu.make_async_copy(res.at[block_of(col), :], xr.at[:, home], loc.at[1])

    here = pl.ds(pl.multiple_of(256 * col, 256), 256)

    def deliver(q, i):
        to = 4 * (q % 2) + i
        return remote(fin.at[q, 32 * i:32 * i + 32, :], out.at[q // 2, :, here], sent.at[6], r6.at[0], row, to)

    def keep(q, i):
        return pltpu.make_async_copy(fin.at[q, 32 * i:32 * i + 32, :], out.at[q // 2, :, here], loc.at[2])

    def send_piece(q, i):
        to = 4 * (q % 2) + i

        @pl.when(col == to)
        def _():
            keep(q, i).start()

        @pl.when(col != to)
        def _():
            deliver(q, i).start()

    @pl.when(root)
    def _():
        for q in range(4):
            own(q).start()
            for p in range(1, 16):
                scatter(q, p).start()

    keep_cols.start()
    keep_rows.start()

    def move(kind, offsets):
        for d in offsets:
            kind(d).start()

    move(move_cols, (1, 7))

    def forward_ring(q):
        @pl.when(zhi == 0)
        def _():
            @pl.when(spot == 0)
            def _():
                own(q).wait()

            @pl.when(spot != 0)
            def _():
                scatter(q, 1).wait_recv()

            for d in range(1, 8):
                along_ring(q, d).start()

    def forward_plane(q):
        @pl.when(zhi == 0)
        def _():
            bulk(g.at[0:3, core, q, mine, :], r2.at[q]).wait_recv()

        @pl.when(zhi != 0)
        def _():
            bulk(g.at[:, core, q, mine, :], r2.at[q]).wait_recv()

        for d in range(1, 16):
            across(q, d).start()

    def swap():
        return remote(half.at[0], half.at[1], s7.at[0], s7.at[1], row, other)

    def gathered(q):
        bulk(g.at[:, core, q, 0:240, :], r3.at[q]).wait_recv()

    def share(q):
        gathered(q)
        to_partner(q).start()

    with jax.named_scope("b_ring0"):
        forward_ring(0)
    with jax.named_scope("b_ring123"):
        for q in range(1, 4):
            forward_ring(q)
    move(move_cols, range(2, 7))
    move(move_rows, range(1, 8))
    with jax.named_scope("c_plane0"):
        forward_plane(0)
    with jax.named_scope("e_plane1"):
        forward_plane(1)
    with jax.named_scope("f_gathered0"):
        gathered(0)

    def arrived():
        keep_cols.wait()
        keep_rows.wait()
        bulk(xf.at[0:896, :], r5.at[0]).wait_recv()
        bulk(xr.at[:, 0:896], r5.at[1]).wait_recv()

    def early_hook(q, i):
        if i == 1:
            with jax.named_scope("j_share"):
                share(q + 1)
        if i == 2:
            @pl.when(q == 1)
            def _():
                with jax.named_scope("j_share3"):
                    share(3)

    def turn(q, carry):
        with jax.named_scope("i_base"):
            base(at, w, sub, lane, lambda i: early_hook(q, i))

        @pl.when(q == 0)
        def _():
            w0[...] = w[...]
            with jax.named_scope("k_chunk01"):
                for s in range(2):
                    to_partner(s).wait_recv()
                    load_chunk(s, g, lf, lr)
            with jax.named_scope("k_second"):
                second_block(w, lf, lr, u01, at, ridge)

        return carry

    def third_hook(i):
        if i == 1:
            for e in range(2):
                for n in range(4):
                    send_piece(e, n)
            to_partner(3).wait_recv()
            load_chunk(3, g, lf, lr)
            lower_panels(w0, w1, u01, lf, lr, xf, xr, aug, ridge, first_col)

    def finish(n):
        rows = slice(32 * n, 32 * n + 32)
        fin[3, rows, :] = hdot(w[rows, :], left[...])

    def last_hook(i):
        if i > 0:
            send_piece(3, i - 1)
        finish(i)
        if i == 3:
            send_piece(3, 3)

    with jax.named_scope("g_half"):
        half[0] = half_block(g, core)
    swap().start()
    to_partner(0).start()
    with jax.named_scope("g_plane23"):
        forward_plane(2)
        forward_plane(3)
    with jax.named_scope("h_swap"):
        swap().wait_recv()
    at[...] = ridged(half[0] + half[1], 0, 0, ridge)
    lax.fori_loop(0, 2, turn, 0)
    w1[...] = w[...]
    with jax.named_scope("l_chunk2"):
        to_partner(2).wait_recv()
        load_chunk(2, g, lf, lr)
    with jax.named_scope("l_third"):
        third_block(w0, w1, u01, lf, lr, aug, at, ridge)
    with jax.named_scope("l_arrived"):
        arrived()
    with jax.named_scope("l_base2"):
        upper_strip(w0, w1, u01, lf, lr, xf, xr, aug, fin, ridge, first_col)
        base(at, w, sub, lane, third_hook)
    with jax.named_scope("m_last"):
        last_panel(w, aug, at, left, fin)
    for n in range(4):
        send_piece(2, n)
    with jax.named_scope("m_base3"):
        base(at, w, sub, lane, last_hook)

    with jax.named_scope("n_final"):
        bulk(fin.at[:, 0:112, :], r6.at[0]).wait_recv()
    with jax.named_scope("o_sends"):
        pltpu.make_async_copy(fin.at[0, 0:64, :], fin.at[1, 0:64, :], loc.at[2]).wait()
        bulk(fin.at[:, 0:112, :], sent.at[6]).wait_send()
        bulk(xf.at[0:896, :], sent.at[4]).wait_send()
        bulk(xr.at[:, 0:896], sent.at[5]).wait_send()
        swap().wait_send()
        bulk(g.at[:, core], sent.at[3]).wait_send()
        bulk(g.at[:, core, :, 0:240, :], sent.at[2]).wait_send()

        @pl.when(zhi == 0)
        def _():
            bulk(g.at[0, core, :, 0:112, :], sent.at[1]).wait_send()

        @pl.when(root)
        def _():
            bulk(g.at[:, core, 0, 0:240, :], sent.at[0]).wait_send()


def local(preacts, resident, ridge):
    dma = pltpu.SemaphoreType.DMA
    raw = pl.pallas_call(
        kernel,
        out_shape=pltpu.VMEM((2, 32, 2048), F32),
        in_specs=[
            pl.BlockSpec(memory_space=pl.ANY),
            pl.BlockSpec(memory_space=pl.ANY),
            pl.BlockSpec(memory_space=pltpu.SMEM),
        ],
        out_specs=pl.BlockSpec(memory_space=pltpu.VMEM),
        scratch_shapes=[
            pltpu.VMEM((4, 2, 4, 256, 128), B16),
            pltpu.VMEM((1024, 256), B16),
            pltpu.VMEM((256, 1024), B16),
            pltpu.VMEM((512, 1024), B16),
            pltpu.VMEM((512, 1024), B16),
            pltpu.VMEM((512, 512), F32),
            pltpu.VMEM((128, 128), F32),
            pltpu.VMEM((2, 128, 128), F32),
            pltpu.VMEM((128, 256), F32),
            pltpu.VMEM((128, 128), F32),
            pltpu.VMEM((128, 128), F32),
            pltpu.VMEM((128, 128), F32),
            pltpu.VMEM((128, 128), F32),
            pltpu.VMEM((4, 128, 256), F32),
            dma((3,)), dma((7,)),
            dma((4,)), dma((4,)), dma((4,)), dma((4,)),
            dma((2,)), dma((1,)), dma((2,)),
        ],
        compiler_params=pltpu.CompilerParams(collective_id=0, has_side_effects=True),
    )(preacts, resident, ridge)
    column = lax.axis_index("row") * 2048 + lax.broadcasted_iota(jnp.int32, raw.shape, 2)
    line = lax.broadcasted_iota(jnp.int32, raw.shape, 0) * 256 + lax.broadcasted_iota(jnp.int32, raw.shape, 1)
    return jnp.where(column >= line + lax.axis_index("col") * 32, raw, 0.0)


def solution(mesh):
    placed = (P("col", "row"), P("row", "col"), P())
    return jax.shard_map(
        local, mesh=mesh, in_specs=placed, out_specs=P(None, "col", "row"), check_vma=False
    )
```

```python
import jax
import jax.numpy as jnp
from jax import lax
from jax.experimental import pallas as pl
from jax.experimental.pallas import tpu as pltpu
from jax.sharding import PartitionSpec as P

HI = lax.Precision.HIGHEST
F32 = jnp.float32
B16 = jnp.bfloat16

def full(x):
    return jnp.broadcast_to(x, (8, 128))

def row_of(x, j):
    return full(x[j:j + 1, :])


def columns(tile, lo):
    return [full(tile[:, lo + j:lo + j + 1]) for j in range(8)]


def base(at, w, sub, lane, hook):
    cb = columns(at[0:8, :], 0)
    for k in range(16):
        lo = 8 * k
        tile = at[lo:lo + 8, :]
        inblk = (lane >= lo) & (lane < lo + 8)
        rows = jnp.where(inblk, jnp.where(lane - lo == sub, 1.0, 0.0), tile)
        wc = [jnp.where(sub == j, 1.0, 0.0).astype(F32) for j in range(8)]
        if k < 15:
            below = at[lo + 8:lo + 16, :]
            first = columns(below, lo)
            nb = columns(below, lo + 8)
            c = list(first)
        piv = []
        diag = jnp.zeros((8, 128), F32)
        for j in range(8):
            d = row_of(cb[j], j)
            p = 1.0 / d
            piv.append(p)
            diag = jnp.where(sub == j, d, diag)
            u = [row_of(cb[j], jj) for jj in range(j + 1, 8)]
            for jj in range(j + 1, 8):
                cb[jj] = cb[jj] - (cb[j] * u[jj - j - 1]) * p
            if k < 15:
                m = c[j] * p
                for jj in range(j + 1, 8):
                    c[jj] = c[jj] - m * u[jj - j - 1]
                for jj in range(8):
                    nb[jj] = nb[jj] - m * row_of(c[j], jj)
            if j < 7:
                m = jnp.where(sub > j, cb[j] * p, 0.0)
                rows = rows - m * row_of(rows, j)
                for jj in range(j + 1):
                    wc[jj] = wc[jj] - m * row_of(wc[jj], j)
        w[lo:lo + 8, :] = jnp.where(lane <= lo + sub, rows, 0.0) * lax.rsqrt(diag)
        if k < 15:
            scaled = [row_of(rows, j) * piv[j] for j in range(8)]
            ys = []
            for j in range(8):
                y = scaled[j]
                for jj in range(j + 1, 8):
                    y = y + row_of(wc[j], jj) * scaled[jj]
                ys.append(y)
            for t in range(k + 1, 16):
                old = at[8 * t:8 * t + 8, :]
                cols = first if t == k + 1 else columns(old, lo)
                parts = [cols[j] * ys[j] for j in range(8)]
                while len(parts) > 1:
                    parts = [a + b for a, b in zip(parts[::2], parts[1::2])]
                at[8 * t:8 * t + 8, :] = jnp.where(inblk, 0.0, old) - parts[0]
            cb = nb
        if k % 4 == 3:
            hook(k // 4)


def hdot(a, b, ca=1, cb=0):
    if b.shape[1 - cb] < 256:
        return lax.dot_general(a, b, (((ca,), (cb,)), ((), ())), precision=HI, preferred_element_type=F32)
    a0, a1, a2 = thirds(a)
    b0, b1, b2 = thirds(b)
    left = jnp.concatenate([a0, a0, a0, a1, a1, a2], axis=ca)
    right = jnp.concatenate([b0, b1, b2, b0, b1, b0], axis=cb)
    return bdot(left, right, ca, cb)


def thirds(x):
    x0 = x.astype(B16)
    rest = x - x0.astype(F32)
    x1 = rest.astype(B16)
    return x0, x1, (rest - x1.astype(F32)).astype(B16)


def bdot(a, b, ca=1, cb=0):
    return lax.dot_general(a, b, (((ca,), (cb,)), ((), ())), preferred_element_type=F32)

def load_chunk(s, g, lf, lr):
    cut = slice(128 * s, 128 * (s + 1))
    for c in range(8):
        lr[cut, 128 * c:128 * (c + 1)] = g[c // 2, c % 2, s, 128:256, :]
        f = jnp.maximum(g[c // 2, c % 2, s, 0:128, :], 0)
        lf[cut, 128 * c:128 * (c + 1)] = f.T


def gram(lf, lr, rows, cols):
    return bdot(lf[rows, :], lf[cols, :], 1, 1) * (1.0 / 1024) - bdot(lr[rows, :], lr[cols, :], 1, 1)


def ridged(x, first_row, first_col, ridge):
    row = lax.broadcasted_iota(jnp.int32, x.shape, 0) + first_row
    col = lax.broadcasted_iota(jnp.int32, x.shape, 1) + first_col
    return x + jnp.where(row == col, ridge, 0.0)


def half_block(g, core):
    total = jnp.zeros((128, 128), F32)
    rest = jnp.zeros((128, 128), F32)
    for z in range(4):
        f = jnp.maximum(g[z, core, 0, 0:128, :], 0)
        r = g[z, core, 0, 128:256, :]
        total = total + bdot(f, f, 0, 0)
        rest = rest + bdot(r, r, 1, 1)
    return total * (1.0 / 1024) - rest


def second_block(w, lf, lr, u01, at, ridge):
    d = gram(lf, lr, slice(0, 256), slice(128, 256))
    x = hdot(w[...], d[:128, :])
    u01[...] = x
    at[...] = ridged(d[128:, :], 0, 0, ridge) - hdot(x, x, 0, 0)


def first_panels(cols, w0, w, u01, aug):
    x0 = hdot(w0[...], aug[0:128, cols])
    x1 = hdot(w[...], aug[128:256, cols] - hdot(u01[...], x0, 0, 0))
    aug[0:128, cols] = x0
    aug[128:256, cols] = x1
    return x0, x1


def half_cols(h):
    return slice(256 + 128 * h, 384 + 128 * h)


def strip(h, rows, lf, lr, xf, xr, aug, ridge, first_col):
    cut = slice(128 * h, 128 * h + 128)
    part = bdot(lf[rows, :], jnp.maximum(xf[:, cut], 0)) * (1.0 / 1024) - bdot(lr[rows, :], xr[cut, :], 1, 1)
    aug[rows, half_cols(h)] = ridged(part, rows.start, first_col + 128 * h, ridge)


def first_row(h, w0, u01, aug, fin):
    cols = half_cols(h)
    x0 = hdot(w0[...], aug[0:128, cols])
    aug[0:128, cols] = x0
    fin[0, :, 128 * h:128 * h + 128] = x0
    aug[128:256, cols] = aug[128:256, cols] - hdot(u01[...], x0, 0, 0)


def second_row(h, w, aug, fin):
    cols = half_cols(h)
    x1 = hdot(w[...], aug[128:256, cols])
    aug[128:256, cols] = x1
    fin[1, :, 128 * h:128 * h + 128] = x1


def third_block(w0, w, u01, lf, lr, aug, at, ridge):
    cols = slice(0, 128)
    aug[0:384, cols] = ridged(gram(lf, lr, slice(0, 384), slice(256, 384)), 0, 256, ridge)
    first_panels(cols, w0, w, u01, aug)
    left = aug[0:256, cols]
    at[...] = aug[256:384, cols] - hdot(left, left, 0, 0)


def last_column(w0, w, u01, lf, lr, aug, ridge):
    cols = slice(128, 256)
    aug[:, cols] = ridged(gram(lf, lr, slice(0, 512), slice(384, 512)), 0, 384, ridge)
    first_panels(cols, w0, w, u01, aug)


def lower_panels(cols, aug):
    aug[256:384, cols] = aug[256:384, cols] - hdot(aug[0:256, 0:128], aug[0:256, cols], 0, 0)
    aug[384:512, cols] = aug[384:512, cols] - hdot(aug[0:256, 128:256], aug[0:256, cols], 0, 0)


def last_panel(w, aug, at, left, fin):
    x = hdot(w[...], aug[256:384, 128:512])
    fin[2] = x[:, 128:384]
    u = x[:, 0:128]
    at[...] = aug[384:512, 128:256] - hdot(u, u, 0, 0)
    left[...] = aug[384:512, 256:512] - hdot(u, x[:, 128:384], 0, 0)


MESH = pl.DeviceIdType.MESH


def remote(src, dst, send, recv, row, col):
    return pltpu.make_async_remote_copy(
        src_ref=src, dst_ref=dst, send_sem=send, recv_sem=recv, device_id=(row, col), device_id_type=MESH
    )


def kernel(pre, res, rd, out, g, xf, xr, lf, lr, aug, u01, half, left, at, w0, w1, w, fin, loc, sent, r1, r2, r3, r4, r5, r6, s7):
    row = lax.axis_index("row")
    col = lax.axis_index("col")
    zhi = lax.rem(row, 2)
    spot = row // 2
    zlo = col // 2
    core = lax.rem(col, 2)
    deep = zhi * 4 + zlo
    other = col + 1 - 2 * core
    ridge = rd[0]
    first_col = row * 2048 + col * 256
    sub = lax.broadcasted_iota(jnp.int32, (8, 128), 0)
    lane = lax.broadcasted_iota(jnp.int32, (8, 128), 1)

    def in_plane(d):
        return 2 * lax.rem(spot + d, 16) + zhi, col

    def in_ring(d):
        z = lax.rem(deep + d, 8)
        return 2 * spot + z // 4, 2 * lax.rem(z, 4) + core

    barrier = pltpu.get_barrier_semaphore()
    peers = [in_plane(d) for d in range(1, 16)] + [in_ring(d) for d in range(1, 8)]
    peers += [(row, 2 * z + 1 - core) for z in range(4)]
    for peer in peers:
        pl.semaphore_signal(barrier, inc=1, device_id=peer, device_id_type=MESH)
    with jax.named_scope("a_barrier"):
        pl.semaphore_wait(barrier, len(peers))

    def piece(q, p):
        if p < 8:
            return pre.at[16 * p:16 * p + 16, 128 * q:128 * q + 128]
        return res.at[128 * q + 16 * (p - 8):128 * q + 16 * (p - 8) + 16, :]

    def scatter(q, p):
        return remote(piece(q, p), g.at[zlo, core, q, 16 * p:16 * p + 16, :], sent.at[0], r1.at[q], 2 * p, col)

    def own(q):
        return pltpu.make_async_copy(piece(q, 0), g.at[zlo, core, q, 0:16, :], r1.at[q])

    mine = pl.ds(pl.multiple_of(16 * spot, 16), 16)

    def along_ring(q, d):
        ref = g.at[zlo, core, q, mine, :]
        return remote(ref, ref, sent.at[1], r2.at[q], *in_ring(d))

    def across(q, d):
        ref = g.at[:, core, q, mine, :]
        return remote(ref, ref, sent.at[2], r3.at[q], *in_plane(d))

    def to_partner(q):
        ref = g.at[:, core, q]
        return remote(ref, ref, sent.at[3], r4.at[q], row, other)

    def bulk(ref, sem):
        return remote(ref, ref, sem, sem, row, other)

    root = (spot == 0) & (zhi == 0)

    home = pl.ds(pl.multiple_of(128 * col, 128), 128)

    def part_of(to, h):
        return pl.ds(pl.multiple_of(256 * to + 128 * h, 128), 128)

    def halves(h):
        cut = slice(128 * h, 128 * h + 128)
        return xf.at[home, cut], xr.at[cut, home]

    def move_cols(h, d):
        to = lax.rem(col + d, 8)
        return remote(pre.at[:, part_of(to, h)], halves(h)[0], sent.at[4], r5.at[2 * h], row, to)

    def move_rows(h, d):
        to = lax.rem(col + d, 8)
        return remote(res.at[part_of(to, h), :], halves(h)[1], sent.at[5], r5.at[2 * h + 1], row, to)

    def stay(h):
        return (
            pltpu.make_async_copy(pre.at[:, part_of(col, h)], halves(h)[0], loc.at[2 * h]),
            pltpu.make_async_copy(res.at[part_of(col, h), :], halves(h)[1], loc.at[2 * h + 1]),
        )

    here = pl.ds(pl.multiple_of(256 * col, 256), 256)

    def deliver(q, i):
        to = 4 * (q % 2) + i
        return remote(fin.at[q, 32 * i:32 * i + 32, :], out.at[q // 2, :, here], sent.at[6], r6.at[0], row, to)

    def keep(q, i):
        return pltpu.make_async_copy(fin.at[q, 32 * i:32 * i + 32, :], out.at[q // 2, :, here], loc.at[4])

    def send_piece(q, i):
        to = 4 * (q % 2) + i

        @pl.when(col == to)
        def _():
            keep(q, i).start()

        @pl.when(col != to)
        def _():
            deliver(q, i).start()

    def send_half(q, h):
        cut = slice(128 * h, 128 * h + 128)
        lanes = pl.ds(pl.multiple_of(256 * col + 128 * h, 128), 128)
        for i in range(4):
            to = 4 * (q % 2) + i
            src = fin.at[q, 32 * i:32 * i + 32, cut]
            dst = out.at[q // 2, :, lanes]

            @pl.when(col == to)
            def _():
                pltpu.make_async_copy(src, dst, loc.at[4]).start()

            @pl.when(col != to)
            def _():
                remote(src, dst, sent.at[6], r6.at[0], row, to).start()

    @pl.when(root)
    def _():
        for q in range(4):
            own(q).start()
            for p in range(1, 16):
                scatter(q, p).start()

    for h in range(2):
        for copy in stay(h):
            copy.start()

    def move(kind, h, offsets):
        for d in offsets:
            kind(h, d).start()

    @pl.when(zhi != 0)
    def _():
        move(move_cols, 0, range(1, 8))
        move(move_rows, 0, range(1, 8))

    @pl.when(zhi == 0)
    def _():
        move(move_cols, 0, (1, 7, 2, 6))

    def forward_ring(q):
        @pl.when(zhi == 0)
        def _():
            @pl.when(spot == 0)
            def _():
                own(q).wait()

            @pl.when(spot != 0)
            def _():
                scatter(q, 1).wait_recv()

            for d in range(1, 8):
                along_ring(q, d).start()

    def forward_plane(q):
        @pl.when(zhi == 0)
        def _():
            bulk(g.at[0:3, core, q, mine, :], r2.at[q]).wait_recv()

        @pl.when(zhi != 0)
        def _():
            bulk(g.at[:, core, q, mine, :], r2.at[q]).wait_recv()

        for d in range(1, 16):
            across(q, d).start()

    def swap():
        return remote(half.at[0], half.at[1], s7.at[0], s7.at[1], row, other)

    def gathered(q):
        bulk(g.at[:, core, q, 0:240, :], r3.at[q]).wait_recv()

    def share(q):
        gathered(q)
        to_partner(q).start()

    with jax.named_scope("b_ring0"):
        forward_ring(0)
    with jax.named_scope("b_ring123"):
        for q in range(1, 4):
            forward_ring(q)

    @pl.when(zhi == 0)
    def _():
        move(move_cols, 0, (3, 4, 5))
        move(move_rows, 0, range(1, 8))

    with jax.named_scope("c_plane0"):
        forward_plane(0)
    with jax.named_scope("e_plane1"):
        forward_plane(1)
    with jax.named_scope("f_gathered0"):
        gathered(0)

    def arrived(h):
        for copy in stay(h):
            copy.wait()
        bulk(xf.at[0:896, 0:128], r5.at[2 * h]).wait_recv()
        bulk(xr.at[0:128, 0:896], r5.at[2 * h + 1]).wait_recv()

    def first_hook(i):
        if i == 1:
            share(1)

    def second_hook(i):
        if i == 0:
            share(2)
        if i == 2:
            share(3)

    def third_hook(i):
        if i == 0:
            arrived(1)
            strip(1, slice(0, 256), lf, lr, xf, xr, aug, ridge, first_col)
            first_row(1, w0, u01, aug, fin)
            second_row(1, w1, aug, fin)
        if i == 1:
            send_half(1, 1)
            send_half(0, 1)
            to_partner(3).wait_recv()
            load_chunk(3, g, lf, lr)
            last_column(w0, w1, u01, lf, lr, aug, ridge)
            strip(0, slice(256, 512), lf, lr, xf, xr, aug, ridge, first_col)
            strip(1, slice(256, 512), lf, lr, xf, xr, aug, ridge, first_col)
            lower_panels(slice(128, 512), aug)

    def finish(n):
        rows = slice(32 * n, 32 * n + 32)
        fin[3, rows, :] = hdot(w[rows, :], left[...])

    def last_hook(i):
        if i > 0:
            send_piece(3, i - 1)
        finish(i)
        if i == 3:
            send_piece(3, 3)

    with jax.named_scope("g_half"):
        half[0] = half_block(g, core)
    swap().start()
    to_partner(0).start()
    with jax.named_scope("g_plane23"):
        forward_plane(2)
        forward_plane(3)
    move(move_cols, 1, range(1, 8))
    move(move_rows, 1, range(1, 8))
    with jax.named_scope("h_swap"):
        swap().wait_recv()
    at[...] = ridged(half[0] + half[1], 0, 0, ridge)
    with jax.named_scope("i_base0"):
        base(at, w, sub, lane, first_hook)
    w0[...] = w[...]
    with jax.named_scope("k_chunk01"):
        for s in range(2):
            to_partner(s).wait_recv()
            load_chunk(s, g, lf, lr)
    with jax.named_scope("k_second"):
        second_block(w, lf, lr, u01, at, ridge)
    with jax.named_scope("k_arrived"):
        arrived(0)
    with jax.named_scope("k_base1"):
        strip(0, slice(0, 256), lf, lr, xf, xr, aug, ridge, first_col)
        first_row(0, w0, u01, aug, fin)
        base(at, w, sub, lane, second_hook)
    w1[...] = w[...]
    second_row(0, w, aug, fin)
    send_half(1, 0)
    send_half(0, 0)
    with jax.named_scope("l_partner2"):
        to_partner(2).wait_recv()
    with jax.named_scope("l_chunk2"):
        load_chunk(2, g, lf, lr)
    with jax.named_scope("l_third"):
        third_block(w0, w1, u01, lf, lr, aug, at, ridge)
    with jax.named_scope("l_base2"):
        base(at, w, sub, lane, third_hook)
    with jax.named_scope("m_last"):
        last_panel(w, aug, at, left, fin)
    for n in range(4):
        send_piece(2, n)
    with jax.named_scope("m_base3"):
        base(at, w, sub, lane, last_hook)

    with jax.named_scope("n_final"):
        bulk(fin.at[:, 0:112, :], r6.at[0]).wait_recv()
    with jax.named_scope("o_sends"):
        pltpu.make_async_copy(fin.at[0, 0:64, :], fin.at[1, 0:64, :], loc.at[4]).wait()
        bulk(fin.at[:, 0:112, :], sent.at[6]).wait_send()
        bulk(xf.at[0:896, :], sent.at[4]).wait_send()
        bulk(xr.at[:, 0:896], sent.at[5]).wait_send()
        swap().wait_send()
        bulk(g.at[:, core], sent.at[3]).wait_send()
        bulk(g.at[:, core, :, 0:240, :], sent.at[2]).wait_send()

        @pl.when(zhi == 0)
        def _():
            bulk(g.at[0, core, :, 0:112, :], sent.at[1]).wait_send()

        @pl.when(root)
        def _():
            bulk(g.at[:, core, 0, 0:240, :], sent.at[0]).wait_send()


def local(preacts, resident, ridge):
    dma = pltpu.SemaphoreType.DMA
    raw = pl.pallas_call(
        kernel,
        out_shape=pltpu.VMEM((2, 32, 2048), F32),
        in_specs=[
            pl.BlockSpec(memory_space=pl.ANY),
            pl.BlockSpec(memory_space=pl.ANY),
            pl.BlockSpec(memory_space=pltpu.SMEM),
        ],
        out_specs=pl.BlockSpec(memory_space=pltpu.VMEM),
        scratch_shapes=[
            pltpu.VMEM((4, 2, 4, 256, 128), B16),
            pltpu.VMEM((1024, 256), B16),
            pltpu.VMEM((256, 1024), B16),
            pltpu.VMEM((512, 1024), B16),
            pltpu.VMEM((512, 1024), B16),
            pltpu.VMEM((512, 512), F32),
            pltpu.VMEM((128, 128), F32),
            pltpu.VMEM((2, 128, 128), F32),
            pltpu.VMEM((128, 256), F32),
            pltpu.VMEM((128, 128), F32),
            pltpu.VMEM((128, 128), F32),
            pltpu.VMEM((128, 128), F32),
            pltpu.VMEM((128, 128), F32),
            pltpu.VMEM((4, 128, 256), F32),
            dma((5,)), dma((7,)),
            dma((4,)), dma((4,)), dma((4,)), dma((4,)),
            dma((4,)), dma((1,)), dma((2,)),
        ],
        compiler_params=pltpu.CompilerParams(collective_id=0, has_side_effects=True),
    )(preacts, resident, ridge)
    column = lax.axis_index("row") * 2048 + lax.broadcasted_iota(jnp.int32, raw.shape, 2)
    line = lax.broadcasted_iota(jnp.int32, raw.shape, 0) * 256 + lax.broadcasted_iota(jnp.int32, raw.shape, 1)
    return jnp.where(column >= line + lax.axis_index("col") * 32, raw, 0.0)


def solution(mesh):
    placed = (P("col", "row"), P("row", "col"), P())
    return jax.shard_map(
        local, mesh=mesh, in_specs=placed, out_specs=P(None, "col", "row"), check_vma=False
    )
```

```python
import jax
import jax.numpy as jnp
from jax import lax
from jax.experimental import pallas as pl
from jax.experimental.pallas import tpu as pltpu
from jax.sharding import PartitionSpec as P

HI = lax.Precision.HIGHEST
F32 = jnp.float32
B16 = jnp.bfloat16

def full(x):
    return jnp.broadcast_to(x, (8, 128))

def row_of(x, j):
    return full(x[j:j + 1, :])


def columns(tile, lo):
    return [full(tile[:, lo + j:lo + j + 1]) for j in range(8)]


def base(at, w, sub, lane, hook):
    cb = columns(at[0:8, :], 0)
    for k in range(16):
        lo = 8 * k
        tile = at[lo:lo + 8, :]
        inblk = (lane >= lo) & (lane < lo + 8)
        rows = jnp.where(inblk, jnp.where(lane - lo == sub, 1.0, 0.0), tile)
        wc = [jnp.where(sub == j, 1.0, 0.0).astype(F32) for j in range(8)]
        if k < 15:
            below = at[lo + 8:lo + 16, :]
            first = columns(below, lo)
            nb = columns(below, lo + 8)
            c = list(first)
        piv = []
        diag = jnp.zeros((8, 128), F32)
        for j in range(8):
            d = row_of(cb[j], j)
            p = 1.0 / d
            piv.append(p)
            diag = jnp.where(sub == j, d, diag)
            u = [row_of(cb[j], jj) for jj in range(j + 1, 8)]
            for jj in range(j + 1, 8):
                cb[jj] = cb[jj] - (cb[j] * u[jj - j - 1]) * p
            if k < 15:
                m = c[j] * p
                for jj in range(j + 1, 8):
                    c[jj] = c[jj] - m * u[jj - j - 1]
                for jj in range(8):
                    nb[jj] = nb[jj] - m * row_of(c[j], jj)
            if j < 7:
                m = jnp.where(sub > j, cb[j] * p, 0.0)
                rows = rows - m * row_of(rows, j)
                for jj in range(j + 1):
                    wc[jj] = wc[jj] - m * row_of(wc[jj], j)
        w[lo:lo + 8, :] = jnp.where(lane <= lo + sub, rows, 0.0) * lax.rsqrt(diag)
        if k < 15:
            scaled = [row_of(rows, j) * piv[j] for j in range(8)]
            ys = []
            for j in range(8):
                y = scaled[j]
                for jj in range(j + 1, 8):
                    y = y + row_of(wc[j], jj) * scaled[jj]
                ys.append(y)
            for t in range(k + 1, 16):
                old = at[8 * t:8 * t + 8, :]
                cols = first if t == k + 1 else columns(old, lo)
                parts = [cols[j] * ys[j] for j in range(8)]
                while len(parts) > 1:
                    parts = [a + b for a, b in zip(parts[::2], parts[1::2])]
                at[8 * t:8 * t + 8, :] = jnp.where(inblk, 0.0, old) - parts[0]
            cb = nb
        if k % 4 == 3:
            hook(k // 4)


def hdot(a, b, ca=1, cb=0):
    if b.shape[1 - cb] < 256:
        return lax.dot_general(a, b, (((ca,), (cb,)), ((), ())), precision=HI, preferred_element_type=F32)
    a0, a1, a2 = thirds(a)
    b0, b1, b2 = thirds(b)
    left = jnp.concatenate([a0, a0, a0, a1, a1, a2], axis=ca)
    right = jnp.concatenate([b0, b1, b2, b0, b1, b0], axis=cb)
    return bdot(left, right, ca, cb)


def thirds(x):
    x0 = x.astype(B16)
    rest = x - x0.astype(F32)
    x1 = rest.astype(B16)
    return x0, x1, (rest - x1.astype(F32)).astype(B16)


def bdot(a, b, ca=1, cb=0):
    return lax.dot_general(a, b, (((ca,), (cb,)), ((), ())), preferred_element_type=F32)

def load_chunk(s, g, lf, lr):
    cut = slice(128 * s, 128 * (s + 1))
    for c in range(8):
        lr[cut, 128 * c:128 * (c + 1)] = g[c // 2, c % 2, s, 128:256, :]
        f = jnp.maximum(g[c // 2, c % 2, s, 0:128, :], 0)
        lf[cut, 128 * c:128 * (c + 1)] = f.T


def gram(lf, lr, rows, cols):
    return bdot(lf[rows, :], lf[cols, :], 1, 1) * (1.0 / 1024) - bdot(lr[rows, :], lr[cols, :], 1, 1)


def ridged(x, first_row, first_col, ridge):
    row = lax.broadcasted_iota(jnp.int32, x.shape, 0) + first_row
    col = lax.broadcasted_iota(jnp.int32, x.shape, 1) + first_col
    return x + jnp.where(row == col, ridge, 0.0)


def half_block(g, core):
    total = jnp.zeros((128, 128), F32)
    rest = jnp.zeros((128, 128), F32)
    for z in range(4):
        f = jnp.maximum(g[z, core, 0, 0:128, :], 0)
        r = g[z, core, 0, 128:256, :]
        total = total + bdot(f, f, 0, 0)
        rest = rest + bdot(r, r, 1, 1)
    return total * (1.0 / 1024) - rest


def second_block(w, lf, lr, u01, at, ridge):
    d = gram(lf, lr, slice(0, 256), slice(128, 256))
    x = hdot(w[...], d[:128, :])
    u01[...] = x
    at[...] = ridged(d[128:, :], 0, 0, ridge) - hdot(x, x, 0, 0)


def first_panels(cols, w0, w, u01, aug):
    x0 = hdot(w0[...], aug[0:128, cols])
    x1 = hdot(w[...], aug[128:256, cols] - hdot(u01[...], x0, 0, 0))
    aug[0:128, cols] = x0
    aug[128:256, cols] = x1
    return x0, x1


def half_cols(h):
    return slice(256 + 128 * h, 384 + 128 * h)


def strip(h, rows, lf, lr, xf, xr, aug, ridge, first_col):
    cut = slice(128 * h, 128 * h + 128)
    part = bdot(lf[rows, :], jnp.maximum(xf[:, cut], 0)) * (1.0 / 1024) - bdot(lr[rows, :], xr[cut, :], 1, 1)
    aug[rows, half_cols(h)] = ridged(part, rows.start, first_col + 128 * h, ridge)


def first_row(h, w0, u01, aug, fin):
    cols = half_cols(h)
    x0 = hdot(w0[...], aug[0:128, cols])
    aug[0:128, cols] = x0
    fin[0, :, 128 * h:128 * h + 128] = x0
    aug[128:256, cols] = aug[128:256, cols] - hdot(u01[...], x0, 0, 0)


def second_row(h, w, aug, fin):
    cols = half_cols(h)
    x1 = hdot(w[...], aug[128:256, cols])
    aug[128:256, cols] = x1
    fin[1, :, 128 * h:128 * h + 128] = x1


def third_block(w0, w, u01, lf, lr, aug, at, ridge):
    cols = slice(0, 128)
    aug[0:384, cols] = ridged(gram(lf, lr, slice(0, 384), slice(256, 384)), 0, 256, ridge)
    first_panels(cols, w0, w, u01, aug)
    left = aug[0:256, cols]
    at[...] = aug[256:384, cols] - hdot(left, left, 0, 0)


def last_column(w0, w, u01, lf, lr, aug, ridge):
    cols = slice(128, 256)
    aug[:, cols] = ridged(gram(lf, lr, slice(0, 512), slice(384, 512)), 0, 384, ridge)
    first_panels(cols, w0, w, u01, aug)


def lower_panels(cols, aug):
    aug[256:384, cols] = aug[256:384, cols] - hdot(aug[0:256, 0:128], aug[0:256, cols], 0, 0)
    aug[384:512, cols] = aug[384:512, cols] - hdot(aug[0:256, 128:256], aug[0:256, cols], 0, 0)


def last_panel(w, aug, at, left, fin):
    x = hdot(w[...], aug[256:384, 128:512])
    fin[2] = x[:, 128:384]
    u = x[:, 0:128]
    at[...] = aug[384:512, 128:256] - hdot(u, u, 0, 0)
    left[...] = aug[384:512, 256:512] - hdot(u, x[:, 128:384], 0, 0)


MESH = pl.DeviceIdType.MESH


def remote(src, dst, send, recv, row, col):
    return pltpu.make_async_remote_copy(
        src_ref=src, dst_ref=dst, send_sem=send, recv_sem=recv, device_id=(row, col), device_id_type=MESH
    )


def kernel(pre, res, rd, out, g, xf, xr, lf, lr, aug, u01, half, left, at, w0, w1, w, fin, loc, sent, r1, r2, r3, r4, r5, r6, s7):
    row = lax.axis_index("row")
    col = lax.axis_index("col")
    zhi = lax.rem(row, 2)
    spot = row // 2
    zlo = col // 2
    core = lax.rem(col, 2)
    deep = zhi * 4 + zlo
    other = col + 1 - 2 * core
    ridge = rd[0]
    first_col = row * 2048 + col * 256
    sub = lax.broadcasted_iota(jnp.int32, (8, 128), 0)
    lane = lax.broadcasted_iota(jnp.int32, (8, 128), 1)

    def in_plane(d):
        return 2 * lax.rem(spot + d, 16) + zhi, col

    def in_ring(d):
        z = lax.rem(deep + d, 8)
        return 2 * spot + z // 4, 2 * lax.rem(z, 4) + core

    barrier = pltpu.get_barrier_semaphore()
    peers = [in_plane(d) for d in range(1, 16)] + [in_ring(d) for d in range(1, 8)]
    peers += [(row, 2 * z + 1 - core) for z in range(4)]
    for peer in peers:
        pl.semaphore_signal(barrier, inc=1, device_id=peer, device_id_type=MESH)
    with jax.named_scope("a_barrier"):
        pl.semaphore_wait(barrier, len(peers))

    def piece(q, p):
        if p < 8:
            return pre.at[16 * p:16 * p + 16, 128 * q:128 * q + 128]
        return res.at[128 * q + 16 * (p - 8):128 * q + 16 * (p - 8) + 16, :]

    def scatter(q, p):
        return remote(piece(q, p), g.at[zlo, core, q, 16 * p:16 * p + 16, :], sent.at[0], r1.at[q], 2 * p, col)

    def own(q):
        return pltpu.make_async_copy(piece(q, 0), g.at[zlo, core, q, 0:16, :], r1.at[q])

    mine = pl.ds(pl.multiple_of(16 * spot, 16), 16)

    def along_ring(q, d):
        ref = g.at[zlo, core, q, mine, :]
        return remote(ref, ref, sent.at[1], r2.at[q], *in_ring(d))

    def across(q, d):
        ref = g.at[:, core, q, mine, :]
        return remote(ref, ref, sent.at[2], r3.at[q], *in_plane(d))

    def to_partner(q):
        ref = g.at[:, core, q]
        return remote(ref, ref, sent.at[3], r4.at[q], row, other)

    def bulk(ref, sem):
        return remote(ref, ref, sem, sem, row, other)

    root = (spot == 0) & (zhi == 0)

    home = pl.ds(pl.multiple_of(128 * col, 128), 128)

    def part_of(to, h):
        return pl.ds(pl.multiple_of(256 * to + 128 * h, 128), 128)

    def halves(h):
        cut = slice(128 * h, 128 * h + 128)
        return xf.at[home, cut], xr.at[cut, home]

    def move_cols(h, d):
        to = lax.rem(col + d, 8)
        return remote(pre.at[:, part_of(to, h)], halves(h)[0], sent.at[4], r5.at[2 * h], row, to)

    def move_rows(h, d):
        to = lax.rem(col + d, 8)
        return remote(res.at[part_of(to, h), :], halves(h)[1], sent.at[5], r5.at[2 * h + 1], row, to)

    def stay(h):
        return (
            pltpu.make_async_copy(pre.at[:, part_of(col, h)], halves(h)[0], loc.at[2 * h]),
            pltpu.make_async_copy(res.at[part_of(col, h), :], halves(h)[1], loc.at[2 * h + 1]),
        )

    here = pl.ds(pl.multiple_of(256 * col, 256), 256)

    def deliver(q, i):
        to = 4 * (q % 2) + i
        return remote(fin.at[q, 32 * i:32 * i + 32, :], out.at[q // 2, :, here], sent.at[6], r6.at[0], row, to)

    def keep(q, i):
        return pltpu.make_async_copy(fin.at[q, 32 * i:32 * i + 32, :], out.at[q // 2, :, here], loc.at[4])

    def send_piece(q, i):
        to = 4 * (q % 2) + i

        @pl.when(col == to)
        def _():
            keep(q, i).start()

        @pl.when(col != to)
        def _():
            deliver(q, i).start()

    def send_half(q, h):
        cut = slice(128 * h, 128 * h + 128)
        lanes = pl.ds(pl.multiple_of(256 * col + 128 * h, 128), 128)
        for i in range(4):
            to = 4 * (q % 2) + i
            src = fin.at[q, 32 * i:32 * i + 32, cut]
            dst = out.at[q // 2, :, lanes]

            @pl.when(col == to)
            def _():
                pltpu.make_async_copy(src, dst, loc.at[4]).start()

            @pl.when(col != to)
            def _():
                remote(src, dst, sent.at[6], r6.at[0], row, to).start()

    @pl.when(root)
    def _():
        for q in range(4):
            own(q).start()
            for p in range(1, 16):
                scatter(q, p).start()

    for h in range(2):
        for copy in stay(h):
            copy.start()

    def move(kind, h, offsets):
        for d in offsets:
            kind(h, d).start()

    @pl.when(zhi != 0)
    def _():
        move(move_cols, 0, range(1, 8))
        move(move_rows, 0, range(1, 8))

    @pl.when(zhi == 0)
    def _():
        move(move_cols, 0, (1, 7, 2, 6))

    def forward_ring(q):
        @pl.when(zhi == 0)
        def _():
            @pl.when(spot == 0)
            def _():
                own(q).wait()

            @pl.when(spot != 0)
            def _():
                scatter(q, 1).wait_recv()

            for d in range(1, 8):
                along_ring(q, d).start()

    def forward_plane(q):
        @pl.when(zhi == 0)
        def _():
            bulk(g.at[0:3, core, q, mine, :], r2.at[q]).wait_recv()

        @pl.when(zhi != 0)
        def _():
            bulk(g.at[:, core, q, mine, :], r2.at[q]).wait_recv()

        for d in range(1, 16):
            across(q, d).start()

    def swap():
        return remote(half.at[0], half.at[1], s7.at[0], s7.at[1], row, other)

    def gathered(q):
        bulk(g.at[:, core, q, 0:240, :], r3.at[q]).wait_recv()

    def share(q):
        gathered(q)
        to_partner(q).start()

    with jax.named_scope("b_ring0"):
        forward_ring(0)
    with jax.named_scope("b_ring123"):
        for q in range(1, 4):
            forward_ring(q)

    @pl.when(zhi == 0)
    def _():
        move(move_cols, 0, (3, 4, 5))
        move(move_rows, 0, range(1, 8))

    with jax.named_scope("c_plane0"):
        forward_plane(0)
    with jax.named_scope("e_plane1"):
        forward_plane(1)
    with jax.named_scope("f_gathered0"):
        gathered(0)

    def arrived(h):
        for copy in stay(h):
            copy.wait()
        bulk(xf.at[0:896, 0:128], r5.at[2 * h]).wait_recv()
        bulk(xr.at[0:128, 0:896], r5.at[2 * h + 1]).wait_recv()

    def first_hook(i):
        if i == 1:
            share(1)

    def second_hook(i):
        if i == 0:
            share(2)
        if i == 2:
            share(3)

    def third_hook(i):
        if i == 0:
            arrived(1)
            strip(1, slice(0, 256), lf, lr, xf, xr, aug, ridge, first_col)
            first_row(1, w0, u01, aug, fin)
            second_row(1, w1, aug, fin)
        if i == 1:
            send_half(1, 1)
            send_half(0, 1)
            strip(0, slice(256, 512), lf, lr, xf, xr, aug, ridge, first_col)
            strip(1, slice(256, 512), lf, lr, xf, xr, aug, ridge, first_col)
            lower_panels(slice(128, 512), aug)

    def finish(n):
        rows = slice(32 * n, 32 * n + 32)
        fin[3, rows, :] = hdot(w[rows, :], left[...])

    def last_hook(i):
        if i > 1:
            send_piece(3, i - 1)
        finish(i)
        if i in (0, 3):
            send_piece(3, i)

    with jax.named_scope("g_half"):
        half[0] = half_block(g, core)
    swap().start()
    to_partner(0).start()
    with jax.named_scope("g_plane23"):
        forward_plane(2)
        forward_plane(3)
    move(move_cols, 1, range(1, 8))
    move(move_rows, 1, range(1, 8))
    with jax.named_scope("h_swap"):
        swap().wait_recv()
    at[...] = ridged(half[0] + half[1], 0, 0, ridge)
    with jax.named_scope("i_base0"):
        base(at, w, sub, lane, first_hook)
    w0[...] = w[...]
    with jax.named_scope("k_chunk01"):
        for s in range(2):
            to_partner(s).wait_recv()
            load_chunk(s, g, lf, lr)
    with jax.named_scope("k_second"):
        second_block(w, lf, lr, u01, at, ridge)
    with jax.named_scope("k_arrived"):
        arrived(0)
    with jax.named_scope("k_base1"):
        strip(0, slice(0, 256), lf, lr, xf, xr, aug, ridge, first_col)
        first_row(0, w0, u01, aug, fin)
        base(at, w, sub, lane, second_hook)
    w1[...] = w[...]
    second_row(0, w, aug, fin)
    send_half(1, 0)
    send_half(0, 0)
    with jax.named_scope("l_partner2"):
        to_partner(2).wait_recv()
    with jax.named_scope("l_chunk2"):
        load_chunk(2, g, lf, lr)
    with jax.named_scope("l_third"):
        third_block(w0, w1, u01, lf, lr, aug, at, ridge)
    with jax.named_scope("l_partner3"):
        to_partner(3).wait_recv()
    with jax.named_scope("l_base2"):
        load_chunk(3, g, lf, lr)
        last_column(w0, w1, u01, lf, lr, aug, ridge)
        base(at, w, sub, lane, third_hook)
    with jax.named_scope("m_last"):
        last_panel(w, aug, at, left, fin)
    for n in range(4):
        send_piece(2, n)
    with jax.named_scope("m_base3"):
        base(at, w, sub, lane, last_hook)

    with jax.named_scope("n_final"):
        bulk(fin.at[:, 0:112, :], r6.at[0]).wait_recv()
    with jax.named_scope("o_sends"):
        pltpu.make_async_copy(fin.at[0, 0:64, :], fin.at[1, 0:64, :], loc.at[4]).wait()
        bulk(fin.at[:, 0:112, :], sent.at[6]).wait_send()
        bulk(xf.at[0:896, :], sent.at[4]).wait_send()
        bulk(xr.at[:, 0:896], sent.at[5]).wait_send()
        swap().wait_send()
        bulk(g.at[:, core], sent.at[3]).wait_send()
        bulk(g.at[:, core, :, 0:240, :], sent.at[2]).wait_send()

        @pl.when(zhi == 0)
        def _():
            bulk(g.at[0, core, :, 0:112, :], sent.at[1]).wait_send()

        @pl.when(root)
        def _():
            bulk(g.at[:, core, 0, 0:240, :], sent.at[0]).wait_send()


def local(preacts, resident, ridge):
    dma = pltpu.SemaphoreType.DMA
    raw = pl.pallas_call(
        kernel,
        out_shape=pltpu.VMEM((2, 32, 2048), F32),
        in_specs=[
            pl.BlockSpec(memory_space=pl.ANY),
            pl.BlockSpec(memory_space=pl.ANY),
            pl.BlockSpec(memory_space=pltpu.SMEM),
        ],
        out_specs=pl.BlockSpec(memory_space=pltpu.VMEM),
        scratch_shapes=[
            pltpu.VMEM((4, 2, 4, 256, 128), B16),
            pltpu.VMEM((1024, 256), B16),
            pltpu.VMEM((256, 1024), B16),
            pltpu.VMEM((512, 1024), B16),
            pltpu.VMEM((512, 1024), B16),
            pltpu.VMEM((512, 512), F32),
            pltpu.VMEM((128, 128), F32),
            pltpu.VMEM((2, 128, 128), F32),
            pltpu.VMEM((128, 256), F32),
            pltpu.VMEM((128, 128), F32),
            pltpu.VMEM((128, 128), F32),
            pltpu.VMEM((128, 128), F32),
            pltpu.VMEM((128, 128), F32),
            pltpu.VMEM((4, 128, 256), F32),
            dma((5,)), dma((7,)),
            dma((4,)), dma((4,)), dma((4,)), dma((4,)),
            dma((4,)), dma((1,)), dma((2,)),
        ],
        compiler_params=pltpu.CompilerParams(collective_id=0, has_side_effects=True),
    )(preacts, resident, ridge)
    column = lax.axis_index("row") * 2048 + lax.broadcasted_iota(jnp.int32, raw.shape, 2)
    line = lax.broadcasted_iota(jnp.int32, raw.shape, 0) * 256 + lax.broadcasted_iota(jnp.int32, raw.shape, 1)
    return jnp.where(column >= line + lax.axis_index("col") * 32, raw, 0.0)


def solution(mesh):
    placed = (P("col", "row"), P("row", "col"), P())
    return jax.shard_map(
        local, mesh=mesh, in_specs=placed, out_specs=P(None, "col", "row"), check_vma=False
    )
```

```python
import jax
import jax.numpy as jnp
from jax import lax
from jax.experimental import pallas as pl
from jax.experimental.pallas import tpu as pltpu
from jax.sharding import PartitionSpec as P

HI = lax.Precision.HIGHEST
F32 = jnp.float32
B16 = jnp.bfloat16

def full(x):
    return jnp.broadcast_to(x, (8, 128))

def row_of(x, j):
    return full(x[j:j + 1, :])


def columns(tile, lo):
    return [full(tile[:, lo + j:lo + j + 1]) for j in range(8)]


def base(at, w, sub, lane, hook):
    cb = columns(at[0:8, :], 0)
    for k in range(16):
        lo = 8 * k
        tile = at[lo:lo + 8, :]
        inblk = (lane >= lo) & (lane < lo + 8)
        rows = jnp.where(inblk, jnp.where(lane - lo == sub, 1.0, 0.0), tile)
        wc = [jnp.where(sub == j, 1.0, 0.0).astype(F32) for j in range(8)]
        if k < 15:
            below = at[lo + 8:lo + 16, :]
            first = columns(below, lo)
            nb = columns(below, lo + 8)
            c = list(first)
        piv = []
        diag = jnp.zeros((8, 128), F32)
        for j in range(8):
            d = row_of(cb[j], j)
            p = 1.0 / d
            piv.append(p)
            diag = jnp.where(sub == j, d, diag)
            u = [row_of(cb[j], jj) for jj in range(j + 1, 8)]
            for jj in range(j + 1, 8):
                cb[jj] = cb[jj] - (cb[j] * u[jj - j - 1]) * p
            if k < 15:
                m = c[j] * p
                for jj in range(j + 1, 8):
                    c[jj] = c[jj] - m * u[jj - j - 1]
                for jj in range(8):
                    nb[jj] = nb[jj] - m * row_of(c[j], jj)
            if j < 7:
                m = jnp.where(sub > j, cb[j] * p, 0.0)
                rows = rows - m * row_of(rows, j)
                for jj in range(j + 1):
                    wc[jj] = wc[jj] - m * row_of(wc[jj], j)
        w[lo:lo + 8, :] = jnp.where(lane <= lo + sub, rows, 0.0) * lax.rsqrt(diag)
        if k < 15:
            scaled = [row_of(rows, j) * piv[j] for j in range(8)]
            ys = []
            for j in range(8):
                y = scaled[j]
                for jj in range(j + 1, 8):
                    y = y + row_of(wc[j], jj) * scaled[jj]
                ys.append(y)
            for t in range(k + 1, 16):
                old = at[8 * t:8 * t + 8, :]
                cols = first if t == k + 1 else columns(old, lo)
                parts = [cols[j] * ys[j] for j in range(8)]
                while len(parts) > 1:
                    parts = [a + b for a, b in zip(parts[::2], parts[1::2])]
                at[8 * t:8 * t + 8, :] = jnp.where(inblk, 0.0, old) - parts[0]
            cb = nb
        if k % 4 == 3:
            hook(k // 4)


def hdot(a, b, ca=1, cb=0):
    if b.shape[1 - cb] < 256:
        return lax.dot_general(a, b, (((ca,), (cb,)), ((), ())), precision=HI, preferred_element_type=F32)
    a0, a1, a2 = thirds(a)
    b0, b1, b2 = thirds(b)
    left = jnp.concatenate([a0, a0, a0, a1, a1, a2], axis=ca)
    right = jnp.concatenate([b0, b1, b2, b0, b1, b0], axis=cb)
    return bdot(left, right, ca, cb)


def thirds(x):
    x0 = x.astype(B16)
    rest = x - x0.astype(F32)
    x1 = rest.astype(B16)
    return x0, x1, (rest - x1.astype(F32)).astype(B16)


def bdot(a, b, ca=1, cb=0):
    return lax.dot_general(a, b, (((ca,), (cb,)), ((), ())), preferred_element_type=F32)

def load_chunk(s, g, lf, lr):
    cut = slice(128 * s, 128 * (s + 1))
    for c in range(8):
        lr[cut, 128 * c:128 * (c + 1)] = g[c // 2, c % 2, s, 128:256, :]
        f = jnp.maximum(g[c // 2, c % 2, s, 0:128, :], 0)
        lf[cut, 128 * c:128 * (c + 1)] = f.T


def gram(lf, lr, rows, cols):
    return bdot(lf[rows, :], lf[cols, :], 1, 1) * (1.0 / 1024) - bdot(lr[rows, :], lr[cols, :], 1, 1)


def ridged(x, first_row, first_col, ridge):
    row = lax.broadcasted_iota(jnp.int32, x.shape, 0) + first_row
    col = lax.broadcasted_iota(jnp.int32, x.shape, 1) + first_col
    return x + jnp.where(row == col, ridge, 0.0)


def half_block(g, core):
    total = jnp.zeros((128, 128), F32)
    rest = jnp.zeros((128, 128), F32)
    for z in range(4):
        f = jnp.maximum(g[z, core, 0, 0:128, :], 0)
        r = g[z, core, 0, 128:256, :]
        total = total + bdot(f, f, 0, 0)
        rest = rest + bdot(r, r, 1, 1)
    return total * (1.0 / 1024) - rest


def second_block(w, lf, lr, u01, at, ridge):
    d = gram(lf, lr, slice(0, 256), slice(128, 256))
    x = hdot(w[...], d[:128, :])
    u01[...] = x
    at[...] = ridged(d[128:, :], 0, 0, ridge) - hdot(x, x, 0, 0)


def first_panels(cols, w0, w, u01, aug):
    x0 = hdot(w0[...], aug[0:128, cols])
    x1 = hdot(w[...], aug[128:256, cols] - hdot(u01[...], x0, 0, 0))
    aug[0:128, cols] = x0
    aug[128:256, cols] = x1
    return x0, x1


def half_cols(h):
    return slice(256 + 128 * h, 384 + 128 * h)


def strip(h, rows, lf, lr, xf, xr, aug, ridge, first_col):
    cut = slice(128 * h, 128 * h + 128)
    part = bdot(lf[rows, :], jnp.maximum(xf[:, cut], 0)) * (1.0 / 1024) - bdot(lr[rows, :], xr[cut, :], 1, 1)
    aug[rows, half_cols(h)] = ridged(part, rows.start, first_col + 128 * h, ridge)


def first_row(h, w0, u01, aug, fin):
    cols = half_cols(h)
    x0 = hdot(w0[...], aug[0:128, cols])
    aug[0:128, cols] = x0
    fin[0, :, 128 * h:128 * h + 128] = x0
    aug[128:256, cols] = aug[128:256, cols] - hdot(u01[...], x0, 0, 0)


def second_row(h, w, aug, fin):
    cols = half_cols(h)
    x1 = hdot(w[...], aug[128:256, cols])
    aug[128:256, cols] = x1
    fin[1, :, 128 * h:128 * h + 128] = x1


def third_block(w0, w, u01, lf, lr, aug, at, ridge):
    cols = slice(0, 128)
    aug[0:384, cols] = ridged(gram(lf, lr, slice(0, 384), slice(256, 384)), 0, 256, ridge)
    first_panels(cols, w0, w, u01, aug)
    left = aug[0:256, cols]
    at[...] = aug[256:384, cols] - hdot(left, left, 0, 0)


def last_column(w0, w, u01, lf, lr, aug, ridge):
    cols = slice(128, 256)
    aug[:, cols] = ridged(gram(lf, lr, slice(0, 512), slice(384, 512)), 0, 384, ridge)
    first_panels(cols, w0, w, u01, aug)


def lower_panels(cols, aug):
    aug[256:384, cols] = aug[256:384, cols] - hdot(aug[0:256, 0:128], aug[0:256, cols], 0, 0)
    aug[384:512, cols] = aug[384:512, cols] - hdot(aug[0:256, 128:256], aug[0:256, cols], 0, 0)


def last_panel(w, aug, at, left, fin):
    x = hdot(w[...], aug[256:384, 128:512])
    fin[2] = x[:, 128:384]
    u = x[:, 0:128]
    at[...] = aug[384:512, 128:256] - hdot(u, u, 0, 0)
    left[...] = aug[384:512, 256:512] - hdot(u, x[:, 128:384], 0, 0)


MESH = pl.DeviceIdType.MESH


def remote(src, dst, send, recv, row, col):
    return pltpu.make_async_remote_copy(
        src_ref=src, dst_ref=dst, send_sem=send, recv_sem=recv, device_id=(row, col), device_id_type=MESH
    )


def kernel(pre, res, rd, out, g, xf, xr, lf, lr, aug, u01, half, left, at, w0, w1, w, fin, loc, sent, r1, r2, r3, r4, r5, r6, s7):
    row = lax.axis_index("row")
    col = lax.axis_index("col")
    zhi = lax.rem(row, 2)
    spot = row // 2
    zlo = col // 2
    core = lax.rem(col, 2)
    deep = zhi * 4 + zlo
    other = col + 1 - 2 * core
    ridge = rd[0]
    first_col = row * 2048 + col * 256
    sub = lax.broadcasted_iota(jnp.int32, (8, 128), 0)
    lane = lax.broadcasted_iota(jnp.int32, (8, 128), 1)

    def in_plane(d):
        return 2 * lax.rem(spot + d, 16) + zhi, col

    def in_ring(d):
        z = lax.rem(deep + d, 8)
        return 2 * spot + z // 4, 2 * lax.rem(z, 4) + core

    barrier = pltpu.get_barrier_semaphore()
    peers = [in_plane(d) for d in range(1, 16)] + [in_ring(d) for d in range(1, 8)]
    peers += [(row, 2 * z + 1 - core) for z in range(4)]
    for peer in peers:
        pl.semaphore_signal(barrier, inc=1, device_id=peer, device_id_type=MESH)
    with jax.named_scope("a_barrier"):
        pl.semaphore_wait(barrier, len(peers))

    def piece(q, p):
        if p < 8:
            return pre.at[16 * p:16 * p + 16, 128 * q:128 * q + 128]
        return res.at[128 * q + 16 * (p - 8):128 * q + 16 * (p - 8) + 16, :]

    def scatter(q, p):
        return remote(piece(q, p), g.at[zlo, core, q, 16 * p:16 * p + 16, :], sent.at[0], r1.at[q], 2 * p, col)

    def own(q):
        return pltpu.make_async_copy(piece(q, 0), g.at[zlo, core, q, 0:16, :], r1.at[q])

    mine = pl.ds(pl.multiple_of(16 * spot, 16), 16)

    def along_ring(q, d):
        ref = g.at[zlo, core, q, mine, :]
        return remote(ref, ref, sent.at[1], r2.at[q], *in_ring(d))

    def across(q, d):
        ref = g.at[:, core, q, mine, :]
        return remote(ref, ref, sent.at[2], r3.at[q], *in_plane(d))

    def to_partner(q):
        ref = g.at[:, core, q]
        return remote(ref, ref, sent.at[3], r4.at[q], row, other)

    def bulk(ref, sem):
        return remote(ref, ref, sem, sem, row, other)

    root = (spot == 0) & (zhi == 0)

    home = pl.ds(pl.multiple_of(128 * col, 128), 128)

    def part_of(to, h):
        return pl.ds(pl.multiple_of(256 * to + 128 * h, 128), 128)

    def halves(h):
        cut = slice(128 * h, 128 * h + 128)
        return xf.at[home, cut], xr.at[cut, home]

    def move_cols(h, d):
        to = lax.rem(col + d, 8)
        return remote(pre.at[:, part_of(to, h)], halves(h)[0], sent.at[4], r5.at[2 * h], row, to)

    def move_rows(h, d):
        to = lax.rem(col + d, 8)
        return remote(res.at[part_of(to, h), :], halves(h)[1], sent.at[5], r5.at[2 * h + 1], row, to)

    def stay(h):
        return (
            pltpu.make_async_copy(pre.at[:, part_of(col, h)], halves(h)[0], loc.at[2 * h]),
            pltpu.make_async_copy(res.at[part_of(col, h), :], halves(h)[1], loc.at[2 * h + 1]),
        )

    here = pl.ds(pl.multiple_of(256 * col, 256), 256)

    def deliver(q, i):
        to = 4 * (q % 2) + i
        return remote(fin.at[q, 32 * i:32 * i + 32, :], out.at[q // 2, :, here], sent.at[6], r6.at[0], row, to)

    def keep(q, i):
        return pltpu.make_async_copy(fin.at[q, 32 * i:32 * i + 32, :], out.at[q // 2, :, here], loc.at[4])

    def send_piece(q, i):
        to = 4 * (q % 2) + i

        @pl.when(col == to)
        def _():
            keep(q, i).start()

        @pl.when(col != to)
        def _():
            deliver(q, i).start()

    def send_half(q, h):
        cut = slice(128 * h, 128 * h + 128)
        lanes = pl.ds(pl.multiple_of(256 * col + 128 * h, 128), 128)
        for i in range(4):
            to = 4 * (q % 2) + i
            src = fin.at[q, 32 * i:32 * i + 32, cut]
            dst = out.at[q // 2, :, lanes]

            @pl.when(col == to)
            def _():
                pltpu.make_async_copy(src, dst, loc.at[4]).start()

            @pl.when(col != to)
            def _():
                remote(src, dst, sent.at[6], r6.at[0], row, to).start()

    @pl.when(root)
    def _():
        for q in range(4):
            own(q).start()
            for p in range(1, 16):
                scatter(q, p).start()

    for h in range(2):
        for copy in stay(h):
            copy.start()

    def move(kind, h, offsets):
        for d in offsets:
            kind(h, d).start()

    @pl.when(zhi != 0)
    def _():
        move(move_cols, 0, range(1, 8))
        move(move_rows, 0, range(1, 8))

    @pl.when(zhi == 0)
    def _():
        move(move_cols, 0, (1, 7, 2, 6))

    def forward_ring(q):
        @pl.when(zhi == 0)
        def _():
            @pl.when(spot == 0)
            def _():
                own(q).wait()

            @pl.when(spot != 0)
            def _():
                scatter(q, 1).wait_recv()

            for d in range(1, 8):
                along_ring(q, d).start()

    def forward_plane(q):
        @pl.when(zhi == 0)
        def _():
            bulk(g.at[0:3, core, q, mine, :], r2.at[q]).wait_recv()

        @pl.when(zhi != 0)
        def _():
            bulk(g.at[:, core, q, mine, :], r2.at[q]).wait_recv()

        for d in range(1, 16):
            across(q, d).start()

    def swap():
        return remote(half.at[0], half.at[1], s7.at[0], s7.at[1], row, other)

    def gathered(q):
        bulk(g.at[:, core, q, 0:240, :], r3.at[q]).wait_recv()

    def share(q):
        gathered(q)
        to_partner(q).start()

    with jax.named_scope("b_ring0"):
        forward_ring(0)
    with jax.named_scope("b_ring123"):
        for q in range(1, 4):
            forward_ring(q)

    @pl.when(zhi == 0)
    def _():
        move(move_cols, 0, (3, 4, 5))
        move(move_rows, 0, range(1, 8))

    with jax.named_scope("c_plane0"):
        forward_plane(0)
    with jax.named_scope("e_plane1"):
        forward_plane(1)
    with jax.named_scope("f_gathered0"):
        gathered(0)

    def arrived(h):
        for copy in stay(h):
            copy.wait()
        bulk(xf.at[0:896, 0:128], r5.at[2 * h]).wait_recv()
        bulk(xr.at[0:128, 0:896], r5.at[2 * h + 1]).wait_recv()

    def first_hook(i):
        if i == 1:
            share(1)

    def second_hook(i):
        if i == 0:
            share(2)
        if i == 2:
            share(3)

    def third_hook(i):
        if i == 0:
            arrived(1)
            strip(1, slice(0, 256), lf, lr, xf, xr, aug, ridge, first_col)
            first_row(1, w0, u01, aug, fin)
            second_row(1, w1, aug, fin)
        if i == 1:
            send_half(1, 1)
            send_half(0, 1)
            strip(1, slice(256, 512), lf, lr, xf, xr, aug, ridge, first_col)
            lower_panels(slice(128, 512), aug)

    def finish(n):
        rows = slice(32 * n, 32 * n + 32)
        fin[3, rows, :] = hdot(w[rows, :], left[...])

    def last_hook(i):
        if i > 1:
            send_piece(3, i - 1)
        finish(i)
        if i in (0, 3):
            send_piece(3, i)

    with jax.named_scope("g_half"):
        half[0] = half_block(g, core)
    swap().start()
    to_partner(0).start()
    with jax.named_scope("g_plane23"):
        forward_plane(2)
        forward_plane(3)
    move(move_cols, 1, range(1, 8))
    move(move_rows, 1, range(1, 8))
    with jax.named_scope("h_swap"):
        swap().wait_recv()
    at[...] = ridged(half[0] + half[1], 0, 0, ridge)
    with jax.named_scope("i_base0"):
        base(at, w, sub, lane, first_hook)
    w0[...] = w[...]
    with jax.named_scope("k_chunk01"):
        for s in range(2):
            to_partner(s).wait_recv()
            load_chunk(s, g, lf, lr)
    with jax.named_scope("k_second"):
        second_block(w, lf, lr, u01, at, ridge)
    with jax.named_scope("k_arrived"):
        arrived(0)
    with jax.named_scope("k_base1"):
        strip(0, slice(0, 256), lf, lr, xf, xr, aug, ridge, first_col)
        first_row(0, w0, u01, aug, fin)
        base(at, w, sub, lane, second_hook)
    w1[...] = w[...]
    second_row(0, w, aug, fin)
    send_half(1, 0)
    send_half(0, 0)
    with jax.named_scope("l_partner2"):
        to_partner(2).wait_recv()
    with jax.named_scope("l_chunk2"):
        load_chunk(2, g, lf, lr)
    with jax.named_scope("l_third"):
        third_block(w0, w1, u01, lf, lr, aug, at, ridge)
    with jax.named_scope("l_partner3"):
        to_partner(3).wait_recv()
    with jax.named_scope("l_base2"):
        load_chunk(3, g, lf, lr)
        last_column(w0, w1, u01, lf, lr, aug, ridge)
        strip(0, slice(256, 512), lf, lr, xf, xr, aug, ridge, first_col)
        base(at, w, sub, lane, third_hook)
    with jax.named_scope("m_last"):
        last_panel(w, aug, at, left, fin)
    for n in range(4):
        send_piece(2, n)
    with jax.named_scope("m_base3"):
        base(at, w, sub, lane, last_hook)

    with jax.named_scope("n_final"):
        bulk(fin.at[:, 0:112, :], r6.at[0]).wait_recv()
    with jax.named_scope("o_sends"):
        pltpu.make_async_copy(fin.at[0, 0:64, :], fin.at[1, 0:64, :], loc.at[4]).wait()
        bulk(fin.at[:, 0:112, :], sent.at[6]).wait_send()
        bulk(xf.at[0:896, :], sent.at[4]).wait_send()
        bulk(xr.at[:, 0:896], sent.at[5]).wait_send()
        swap().wait_send()
        bulk(g.at[:, core], sent.at[3]).wait_send()
        bulk(g.at[:, core, :, 0:240, :], sent.at[2]).wait_send()

        @pl.when(zhi == 0)
        def _():
            bulk(g.at[0, core, :, 0:112, :], sent.at[1]).wait_send()

        @pl.when(root)
        def _():
            bulk(g.at[:, core, 0, 0:240, :], sent.at[0]).wait_send()


def local(preacts, resident, ridge):
    dma = pltpu.SemaphoreType.DMA
    raw = pl.pallas_call(
        kernel,
        out_shape=pltpu.VMEM((2, 32, 2048), F32),
        in_specs=[
            pl.BlockSpec(memory_space=pl.ANY),
            pl.BlockSpec(memory_space=pl.ANY),
            pl.BlockSpec(memory_space=pltpu.SMEM),
        ],
        out_specs=pl.BlockSpec(memory_space=pltpu.VMEM),
        scratch_shapes=[
            pltpu.VMEM((4, 2, 4, 256, 128), B16),
            pltpu.VMEM((1024, 256), B16),
            pltpu.VMEM((256, 1024), B16),
            pltpu.VMEM((512, 1024), B16),
            pltpu.VMEM((512, 1024), B16),
            pltpu.VMEM((512, 512), F32),
            pltpu.VMEM((128, 128), F32),
            pltpu.VMEM((2, 128, 128), F32),
            pltpu.VMEM((128, 256), F32),
            pltpu.VMEM((128, 128), F32),
            pltpu.VMEM((128, 128), F32),
            pltpu.VMEM((128, 128), F32),
            pltpu.VMEM((128, 128), F32),
            pltpu.VMEM((4, 128, 256), F32),
            dma((5,)), dma((7,)),
            dma((4,)), dma((4,)), dma((4,)), dma((4,)),
            dma((4,)), dma((1,)), dma((2,)),
        ],
        compiler_params=pltpu.CompilerParams(collective_id=0, has_side_effects=True),
    )(preacts, resident, ridge)
    column = lax.axis_index("row") * 2048 + lax.broadcasted_iota(jnp.int32, raw.shape, 2)
    line = lax.broadcasted_iota(jnp.int32, raw.shape, 0) * 256 + lax.broadcasted_iota(jnp.int32, raw.shape, 1)
    return jnp.where(column >= line + lax.axis_index("col") * 32, raw, 0.0)


def solution(mesh):
    placed = (P("col", "row"), P("row", "col"), P())
    return jax.shard_map(
        local, mesh=mesh, in_specs=placed, out_specs=P(None, "col", "row"), check_vma=False
    )
```
